512 devices in a mesh: basis: 16 (over x, y), docs: 32 (over z, core).
Axes of the slice: x: 4, y: 4, z: 16, core: 2. Of those that a mesh axis runs over, the one named last changes fastest.
Arguments:
- eig_in: bfloat16 [28672, 28672], P('basis', 'docs'), may hold values from -0.03125 to 0.03125
- eig_out: bfloat16 [8192, 8192], P('basis', 'docs'), may hold values from -0.0625 to 0.0625
- eigvals: bfloat16 [8192, 28672], P('basis', 'docs'), may hold values from 0.0025 to 3.6
- out_factors: bfloat16 [8192, 256], P('docs'), may hold values from -1.1953125 to 1.1953125
- in_factors: bfloat16 [28672, 256], P(('basis', 'docs')), may hold values from -1.1953125 to 1.1953125
- test_matrix: bfloat16 [28672, 32], P('docs'), may hold values from -0.03125 to 0.03125
- activations: bfloat16 [4096, 28672], P('docs', 'basis'), may hold values from -6 to 6
- gradients: bfloat16 [4096, 8192], P('docs', 'basis'), may hold values from -0.00059890747 to 0.00059890747
- doc_lengths: int32 [128], replicated, may hold values from 1 to 96, 4096 in all
Outputs:
- scores: float32 [4096, 4], P('docs')
- doc_influence: float32 [128, 4], replicated
The draws below stay inside these ranges and needn't reach their ends.
Inputs may be any that keep to these rules, and one draw needn't show every extreme that they name: `doc_lengths`: the documents lie end to end in token order and their lengths sum to 4096.
All inputs are finite; a program needn't handle non-finite values.
Results may differ from the reference program's by a relative error of at most 0.0085.
Values may be sent and summed in bfloat16 or wider, within the bound.
A program may use at most 64 MiB of HBM per device.

```python
import math
import jax
import jax.numpy as jnp
import numpy as np
from jax import lax

D = 8192
FF = 28672
QUERIES = 4
LQ = 64
RANK = 32
TOKENS = 4096
DOCUMENTS = 128
DOC_MOST = 96
QCOLS = 256


def draw_eigvals(key, part):
    row_place = jnp.arange(D, dtype=jnp.float32)[:, None] / D
    col_place = jnp.arange(FF, dtype=jnp.float32)[None, :] / FF
    rough_part = jax.random.uniform(key, (D, FF), jnp.float32, 0.3, 1.7)
    profile = jnp.exp(-3.0 * row_place - 2.0 * col_place)
    return (2.0 * profile * rough_part).astype(jnp.bfloat16)


def block_levels(key, extent, shards, smallest, high):
    def one(dim, parts):
        steps = jax.random.uniform(jax.random.fold_in(jax.random.fold_in(key, 6), dim), (parts,), jnp.float32, smallest / len(shards), high / len(shards))
        return jnp.repeat(jnp.exp(steps), extent[dim] // parts).reshape((-1,) + (1,) * (len(extent) - dim - 1))

    level = one(*shards[0])
    for cut in shards[1:]:
        level = level * one(*cut)
    return level


def split_up(number_of, total, limit, lean):
    portions = [(1 << 20) // math.isqrt(standing ** lean) + 1 for standing in range(2, number_of + 1)]
    surplus, counts = total - limit - (number_of - 1), [1] * (number_of - 1)
    while surplus > 0:
        candidates = [i for i in range(number_of - 1) if counts[i] < limit]
        whole, budget = sum([portions[i] for i in candidates]), surplus
        for i in candidates:
            more = min(limit - counts[i], max(1, budget * portions[i] // whole), surplus)
            counts[i] = counts[i] + more
            surplus = surplus - more
    return np.array([limit] + counts)


def ragged_sizes(own_key, amount, total, limit, slope):
    if amount == 2:
        one = jax.random.randint(own_key, (), max(1, total - limit), min(limit, total - 1) + 1)
        return jnp.stack([one, total - one])
    lengths = jnp.asarray(split_up(amount, total, limit, slope), jnp.int32)
    twos = (amount - 1) // 2
    source_of, sink = lengths[1:1 + 2 * twos:2], lengths[2:2 + 2 * twos:2]
    slack = jnp.minimum(source_of - 1, limit - sink)
    passed = jax.random.randint(jax.random.fold_in(own_key, 1), (twos,), 0, 1 << 20) % (slack + 1)
    lengths = lengths.at[1:1 + 2 * twos:2].set(source_of - passed).at[2:2 + 2 * twos:2].set(sink + passed)
    return lengths[jax.random.permutation(jax.random.fold_in(own_key, 2), amount)]


def gaussian(own_key, shape, deviation, limit, shards=(), kind=jnp.bfloat16):
    values = jax.random.normal(own_key, shape, jnp.float32) * deviation
    if len(shards) > 0:
        values = block_levels(own_key, shape, shards, -0.22, 0.18) * values
    return jnp.clip(values, min=-limit, max=limit).astype(kind)


def setup_inputs(seed: int = 0) -> dict:
    streams_of = jax.random.split(jax.random.key(seed), 10)
    eig_in = gaussian(streams_of[0], (FF, FF), FF ** -0.5, 0.03125, ((0, 16), (1, 32)))
    eig_out = gaussian(streams_of[1], (D, D), D ** -0.5, 0.0625, ((0, 16), (1, 32)))
    eigvals = draw_eigvals(jax.random.fold_in(streams_of[9], 71), 0)
    out_factors = gaussian(streams_of[3], (D, QCOLS), 0.2, 1.1953125, ((0, 32),))
    in_factors = gaussian(streams_of[4], (FF, QCOLS), 0.2, 1.1953125, ((0, 512),))
    test_matrix = gaussian(streams_of[5], (FF, RANK), FF ** -0.5, 0.03125, ((0, 32),))
    activations = gaussian(streams_of[6], (TOKENS, FF), 1.0, 6.0, ((0, 32), (1, 16)))
    gradients = gaussian(streams_of[7], (TOKENS, D), 0.0001, 0.00059890747, ((0, 32), (1, 16)))
    doc_lengths = ragged_sizes(streams_of[8], DOCUMENTS, TOKENS, DOC_MOST, 2).astype(jnp.int32)
    return dict(eig_in=eig_in, eig_out=eig_out, eigvals=eigvals, out_factors=out_factors, in_factors=in_factors, test_matrix=test_matrix, activations=activations, gradients=gradients, doc_lengths=doc_lengths)


damping = 0.1
highest = lax.Precision.HIGHEST

def reference(eig_in, eig_out, eigvals, out_factors, in_factors, test_matrix, activations, gradients, doc_lengths):
    rot_out = jnp.dot(eig_out.astype(jnp.float32), out_factors.astype(jnp.float32), preferred_element_type=jnp.float32).astype(jnp.bfloat16)
    rot_in = lax.dot_general(eig_in.astype(jnp.float32), in_factors.astype(jnp.float32), (((0,), (0,)), ((), ())), preferred_element_type=jnp.float32).astype(jnp.bfloat16)
    out_split = jnp.transpose(rot_out.reshape(D, QUERIES, LQ), (1, 0, 2))
    in_split = jnp.transpose(rot_in.reshape(FF, QUERIES, LQ), (1, 0, 2))
    test_wide = test_matrix.astype(jnp.float32)

    def one_query(query_pair):
        out_rows, in_rows = query_pair
        weight = 1.0 / (eigvals.astype(jnp.float32) + damping)
        moment = lax.dot_general(out_rows.astype(jnp.float32), in_rows.astype(jnp.float32), (((1,), (1,)), ((), ())), preferred_element_type=jnp.float32) * weight
        sketch = lax.dot_general(test_wide, moment, (((0,), (1,)), ((), ())), precision=highest)
        gram_total = jnp.dot(sketch, sketch.T, precision=highest)
        lower_factor = jnp.linalg.cholesky(gram_total)
        range_rows = lax.linalg.triangular_solve(lower_factor, sketch, left_side=True, lower=True)
        projected = jnp.dot(range_rows, moment, precision=highest).astype(jnp.bfloat16)
        return (range_rows, projected)
    range_all, projected_all = lax.map(one_query, (out_split, in_split))
    right_factor = lax.dot_general(eig_in.astype(jnp.float32), projected_all.reshape(QUERIES * RANK, FF).astype(jnp.float32), (((1,), (1,)), ((), ())), preferred_element_type=jnp.float32).astype(jnp.bfloat16)
    left_factor = lax.dot_general(eig_out.astype(jnp.float32), range_all.reshape(QUERIES * RANK, D), (((0,), (1,)), ((), ())), precision=highest).astype(jnp.bfloat16)
    token_in = jnp.dot(activations.astype(jnp.float32), right_factor.astype(jnp.float32), preferred_element_type=jnp.float32)
    token_out = jnp.dot(gradients.astype(jnp.float32), left_factor.astype(jnp.float32), preferred_element_type=jnp.float32)
    scores = (token_in * token_out).reshape(TOKENS, QUERIES, RANK).sum(axis=2)
    doc_ends = jnp.cumsum(doc_lengths).astype(jnp.int32)
    doc_starts = doc_ends - doc_lengths.astype(jnp.int32)
    positions = jnp.arange(TOKENS, dtype=jnp.int32)
    member = ((positions[:, None] >= doc_starts[None, :]) & (positions[:, None] < doc_ends[None, :])).astype(jnp.float32)
    doc_influence = lax.dot_general(member, scores, (((0,), (0,)), ((), ())), precision=highest)
    return (scores, doc_influence)
```

```python
import functools

import jax
import jax.numpy as jnp
from jax import lax
from jax.experimental import pallas as pl
from jax.experimental.pallas import tpu as pltpu
from jax.sharding import PartitionSpec as P

QUERIES = 4
LQ = 64
RANK = 32
QR = QUERIES * RANK
QC = QUERIES * LQ
DAMPING = 0.1
MESH = pl.DeviceIdType.MESH
HIGHEST = lax.Precision.HIGHEST
F32 = jnp.float32
BF16 = jnp.bfloat16


def nn(a, b, precision=None):
    return lax.dot_general(a, b, (((1,), (0,)), ((), ())), precision=precision, preferred_element_type=F32)


def nt(a, b, precision=None):
    return lax.dot_general(a, b, (((1,), (1,)), ((), ())), precision=precision, preferred_element_type=F32)


def tn(a, b, precision=None):
    return lax.dot_general(a, b, (((0,), (0,)), ((), ())), precision=precision, preferred_element_type=F32)


def iota(shape, axis):
    return lax.broadcasted_iota(jnp.int32, shape, axis)


def near_first(n):
    order = []
    for k in range(1, n // 2 + 1):
        order.append(k)
        if n - k != k:
            order.append(n - k)
    return order


def wait_bytes(ref, sem):
    pltpu.make_async_copy(ref, ref, sem).wait()


def body(
    nb,
    nz,
    ein_h,
    eout_h,
    lam_h,
    of_h,
    inf_h,
    te_h,
    act_h,
    gr_h,
    len_h,
    scores_o,
    doc_o,
    ein,
    eout,
    lam,
    outf,
    te,
    act,
    gr,
    lens,
    xin,
    acc,
    wgt,
    tsel,
    mom,
    pin_s,
    pin_r,
    rin,
    po_s,
    po_p,
    po_z,
    po_r,
    ro,
    sk_s,
    sk_p,
    sk_z,
    sk_r,
    sk,
    gm_s,
    gm_r,
    pj_s,
    pj_r,
    pj,
    lf_s,
    lf_r,
    lf_c,
    lf,
    rt_s,
    rt_p,
    rt_z,
    rt_r,
    rt,
    tk_s,
    tk_r,
    sc,
    dc_s,
    dc_p,
    dc_z,
    dc_r,
    in_sem,
    a_send,
    a_recv,
    f_send,
    f_recv,
    sends,
    recvs,
):
    b = lax.axis_index("basis")
    d = lax.axis_index("docs")
    z = lax.div(d, 2)
    c = lax.rem(d, 2)
    mate = {"docs": z * 2 + (1 - c)}
    sent = []

    def zdev(k):
        return {"docs": lax.rem(z + k, nz) * 2 + c}

    def bdev(k):
        return {"basis": lax.rem(b + k, nb)}

    def put(src, dst, s, r, dev):
        pltpu.make_async_remote_copy(
            src_ref=src, dst_ref=dst, send_sem=s, recv_sem=r, device_id=dev, device_id_type=MESH
        ).start()

    def to_mate(src, dst, ch):
        put(src, dst, sends.at[ch], recvs.at[ch], mate)
        sent.append((src, sends.at[ch]))

    def scatter(n, dev, me, src, base, dst, ch):
        for k in near_first(n):
            put(
                src.at[base + lax.rem(me + k, n)],
                dst.at[k],
                sends.at[ch],
                recvs.at[ch],
                dev(k),
            )
        sent.append((dst.at[pl.ds(0, n - 1)], sends.at[ch]))

    def spread(n, dev, ref, where, ch):
        for k in near_first(n):
            put(ref.at[where], ref.at[where], sends.at[ch], recvs.at[ch], dev(k))
        sent.append((ref.at[pl.ds(0, n - 1)], sends.at[ch]))

    def arrived(n, ref, ch):
        wait_bytes(ref.at[pl.ds(0, n - 1)], recvs.at[ch])

    def added(n, first, ref):
        total = first.astype(F32)
        for k in range(1, n):
            total = total + ref[k].astype(F32)
        return total

    loads = []
    for i, (src, dst) in enumerate(
        (
            (inf_h, xin.at[d]),
            (eout_h, eout),
            (of_h, outf),
            (ein_h, ein),
            (lam_h, lam),
            (te_h, te),
            (act_h, act),
            (gr_h, gr),
            (len_h, lens),
        )
    ):
        cp = pltpu.make_async_copy(src, dst, in_sem.at[i])
        cp.start()
        loads.append(cp)

    barrier = pltpu.get_barrier_semaphore()
    for k in near_first(nz):
        pl.semaphore_signal(barrier, inc=1, device_id=zdev(k), device_id_type=MESH)
    for k in near_first(nb):
        pl.semaphore_signal(barrier, inc=1, device_id=bdev(k), device_id_type=MESH)
    pl.semaphore_signal(barrier, inc=1, device_id=mate, device_id_type=MESH)
    twin = {"basis": z, "docs": b * 2 + c}

    @pl.when(b != z)
    def _():
        pl.semaphore_signal(barrier, inc=1, device_id=twin, device_id_type=MESH)

    pl.semaphore_wait(barrier, nz + nb - 1 + jnp.where(b != z, 1, 0))

    loads[0].wait()
    for k in near_first(nz):
        put(xin.at[d], xin.at[d], a_send, a_recv.at[k], zdev(k))
    sent.append((xin.at[pl.ds(0, nz - 1)], a_send))
    put(xin.at[d], xin.at[d], f_send, f_recv.at[0], mate)

    loads[1].wait()
    loads[2].wait()
    part = nn(eout[...], outf[...])
    po_s[...] = part.astype(BF16).reshape(po_s.shape)
    to_mate(po_s.at[pl.ds((1 - c) * nz, nz)], po_p, 0)

    loads[4].wait()
    wgt[...] = 1.0 / (lam[...].astype(F32) + DAMPING)
    loads[5].wait()
    wide = jnp.concatenate([te[...].astype(F32)] * QUERIES, axis=1)
    for q in range(QUERIES):
        tsel[q] = jnp.where(lax.div(iota(wide.shape, 1), RANK) == q, wide, 0.0).astype(BF16)

    wait_bytes(po_p, recvs.at[0])
    po_z[...] = (po_s[pl.ds(c * nz, nz)].astype(F32) + po_p[...].astype(F32)).astype(BF16)

    for k in near_first(nz):
        origin = lax.rem(z - k + nz, nz) * 2 + c
        pltpu.make_async_copy(xin.at[origin], xin.at[origin], a_recv.at[k]).wait()
        put(xin.at[origin], xin.at[origin], f_send, f_recv.at[k], mate)
    sent.append((xin.at[pl.ds(0, nz)], f_send))
    scatter(nz, zdev, z, po_z, 0, po_r, 1)
    for k in range(nz):
        other = lax.rem(z - k + nz, nz) * 2 + 1 - c
        pltpu.make_async_copy(xin.at[other], xin.at[other], f_recv.at[k]).wait()

    loads[3].wait()
    pieces = xin.shape[0] // 4
    rows = pieces * xin.shape[1]
    for i in range(4):
        x = xin[pl.ds(i * pieces, pieces)].astype(F32).reshape(rows, QC).astype(BF16)
        t = tn(x, ein[pl.ds(i * rows, rows), :])
        if i == 0:
            acc[...] = t
        elif i < 3:
            acc[...] += t
        else:
            t = acc[...] + t
            pin_s[...] = t.astype(BF16).reshape(pin_s.shape)
    scatter(nb, bdev, b, pin_s, 0, pin_r, 2)

    arrived(nz, po_r, 1)
    ro[c * nz + z] = added(nz, po_z[z], po_r).astype(BF16)
    spread(nz, zdev, ro, c * nz + z, 3)

    arrived(nb, pin_r, 2)
    rin[b] = added(nb, pin_s[b], pin_r).astype(BF16)
    spread(nb, bdev, rin, b, 4)

    arrived(nz, ro, 3)
    to_mate(ro.at[pl.ds(c * nz, nz)], ro.at[pl.ds(c * nz, nz)], 5)
    wait_bytes(ro.at[pl.ds(0, nz)], recvs.at[5])
    arrived(nb, rin, 4)

    rows_out = eout.shape[0]
    cols_in = ein.shape[1]
    rotin = rin[...].reshape(QC, cols_in)
    rotout = ro[...].reshape(rows_out, QC)
    step = 128
    per = sk_s.shape[1]
    for i in range(rows_out // step):
        block = rotout[i * step : (i + 1) * step, :]
        lane = lax.div(iota(block.shape, 1), LQ)
        total = None
        for q in range(QUERIES):
            only = jnp.where(lane == q, block.astype(F32), 0.0).astype(BF16)
            m = (nn(only, rotin) * wgt[pl.ds(i * step, step), :]).astype(BF16)
            mom[q, pl.ds(i * step, step), :] = m
            t = nn(m, tsel[q])
            total = t if total is None else total + t
        sk_s[pl.ds(i * step // per, step // per)] = total.astype(BF16).reshape(step // per, per, QR)
    to_mate(sk_s.at[pl.ds((1 - c) * nz, nz)], sk_p, 6)
    wait_bytes(sk_p, recvs.at[6])
    sk_z[...] = (sk_s[pl.ds(c * nz, nz)].astype(F32) + sk_p[...].astype(F32)).astype(BF16)
    scatter(nz, zdev, z, sk_z, 0, sk_r, 7)
    arrived(nz, sk_r, 7)
    sk[c * nz + z] = added(nz, sk_z[z], sk_r).astype(BF16)
    spread(nz, zdev, sk, c * nz + z, 8)
    arrived(nz, sk, 8)
    to_mate(sk.at[pl.ds(c * nz, nz)], sk.at[pl.ds(c * nz, nz)], 9)
    wait_bytes(sk.at[pl.ds(0, nz)], recvs.at[9])

    sketch = sk[...].reshape(rows_out, QR).astype(F32).T.astype(BF16)
    gram = nt(sketch, sketch)
    lane_q = lax.div(iota((RANK, QR), 1), RANK)
    mine = jnp.zeros((RANK, QR), F32)
    for q in range(QUERIES):
        mine = mine + jnp.where(lane_q == q, gram[q * RANK : (q + 1) * RANK, :], 0.0)
    gm_s[...] = mine
    for k in near_first(nb):
        put(gm_s, gm_r.at[k], sends.at[10], recvs.at[10], bdev(k))
    sent.append((gm_r.at[pl.ds(0, nb - 1)], sends.at[10]))

    raw = jnp.concatenate(
        [nn(sketch[q * RANK : (q + 1) * RANK, :], mom[q]) for q in range(QUERIES)], axis=0
    )
    acc[pl.ds(0, QR), :] = raw
    left_raw = nn(sketch, eout[...])

    arrived(nb, gm_r, 10)
    a0 = added(nb, mine, gm_r)
    row = iota((RANK, QR), 0)
    lane = iota((RANK, QR), 1)
    in_q = lane - lane_q * RANK

    def over_lanes(x):
        out = jnp.zeros((RANK, QR), F32)
        for q in range(QUERIES):
            s = jnp.sum(jnp.where(lane_q == q, x, 0.0), axis=1, keepdims=True)
            out = jnp.where(lane_q == q, s, out)
        return out

    def eliminate(k, carry):
        a, e = carry
        col = over_lanes(jnp.where(in_q == k, a, 0.0))
        at = row == k
        pivot = jnp.sum(jnp.where(at, col, 0.0), axis=0, keepdims=True)
        row_a = jnp.sum(jnp.where(at, a, 0.0), axis=0, keepdims=True)
        row_e = jnp.sum(jnp.where(at, e, 0.0), axis=0, keepdims=True)
        f = jnp.where(row > k, col / pivot, 0.0)
        return a - f * row_a, e - f * row_e

    e0 = jnp.where(in_q == row, 1.0, 0.0).astype(F32)
    a1, e1 = lax.fori_loop(0, RANK, eliminate, (a0, e0))
    inv = e1 / jnp.sqrt(over_lanes(jnp.where(in_q == row, a1, 0.0)))
    tall = jnp.concatenate([inv] * QUERIES, axis=0)
    same = lax.div(iota((QR, QR), 0), RANK) == lax.div(iota((QR, QR), 1), RANK)
    solve = jnp.where(same, tall, 0.0)

    pj_s[...] = nn(solve, acc[pl.ds(0, QR), :], HIGHEST).reshape(pj_s.shape).astype(BF16)
    scatter(nb, bdev, b, pj_s, 0, pj_r, 11)
    lf_s[...] = nn(solve, left_raw, HIGHEST).T.reshape(lf_s.shape).astype(BF16)
    scatter(nb, bdev, b, lf_s, 0, lf_r, 12)
    arrived(nb, pj_r, 11)
    pj[b] = added(nb, pj_s[b], pj_r).astype(BF16)
    spread(nb, bdev, pj, b, 13)
    arrived(nb, lf_r, 12)
    left_here = added(nb, lf_s[b], lf_r).astype(BF16)
    lf_c[...] = left_here

    @pl.when(b == z)
    def _():
        lf[c * nz + z] = left_here

    @pl.when(b != z)
    def _():
        put(lf_c, lf.at[c * nz + b], sends.at[14], recvs.at[14], twin)

    arrived(nb, pj, 13)
    proj = pj[...].astype(F32).reshape(QR, cols_in).astype(BF16)

    slots = rt_s.shape[0] // 4
    tall_rows = slots * rt_s.shape[1]
    for i in range(4):
        r = nt(ein[pl.ds(i * tall_rows, tall_rows), :], proj)
        rt_s[pl.ds(i * slots, slots)] = r.reshape(slots, rt_s.shape[1], QR).astype(BF16)
    to_mate(rt_s.at[pl.ds((1 - c) * nz, nz)], rt_p, 15)
    wait_bytes(rt_p, recvs.at[15])
    rt_z[...] = (rt_s[pl.ds(c * nz, nz)].astype(F32) + rt_p[...].astype(F32)).astype(BF16)
    scatter(nz, zdev, z, rt_z, 0, rt_r, 16)

    @pl.when(b != z)
    def _():
        wait_bytes(lf_c, recvs.at[14])
        wait_bytes(lf_c, sends.at[14])

    spread(nz, zdev, lf, c * nz + z, 17)
    arrived(nz, rt_r, 16)
    rt[c * nz + z] = added(nz, rt_z[z], rt_r).astype(BF16)
    spread(nz, zdev, rt, c * nz + z, 18)
    arrived(nz, lf, 17)
    to_mate(lf.at[pl.ds(c * nz, nz)], lf.at[pl.ds(c * nz, nz)], 19)
    arrived(nz, rt, 18)
    to_mate(rt.at[pl.ds(c * nz, nz)], rt.at[pl.ds(c * nz, nz)], 20)

    loads[6].wait()
    loads[7].wait()
    loads[8].wait()
    wait_bytes(lf.at[pl.ds(0, nz)], recvs.at[19])
    left = lf[...].astype(F32).reshape(gr.shape[1], QR).astype(BF16)
    tk_s[:, :, QR:] = nn(gr[...], left).reshape(nb, -1, QR)
    half = act.shape[1] // 2
    tokens = act.shape[0]
    wait_bytes(rt.at[pl.ds(0, nz)], recvs.at[20])
    tok = None
    for i in range(2):
        right = rt[pl.ds(i * nz, nz)].astype(F32).reshape(half, QR).astype(BF16)
        t = nn(act[:, i * half : (i + 1) * half], right)
        tok = t if tok is None else tok + t
    tk_s[:, :, :QR] = tok.reshape(nb, -1, QR)
    scatter(nb, bdev, b, tk_s, 0, tk_r, 21)

    here = d * tokens + iota((tokens, lens.shape[1]), 0)
    length = lens[...].astype(F32)
    earlier = jnp.where(
        iota((lens.shape[1],) * 2, 0) < iota((lens.shape[1],) * 2, 1), 1.0, 0.0
    ).astype(BF16)
    start = nn(jnp.broadcast_to(length, (8, lens.shape[1])).astype(BF16), earlier)[0:1, :]
    stop = start + length
    place = here.astype(F32)
    member = jnp.where((place >= start) & (place < stop), 1.0, 0.0).astype(F32)
    pick = jnp.where(
        lax.div(iota((QR, 128), 0), RANK) == iota((QR, 128), 1), 1.0, 0.0
    ).astype(F32)

    arrived(nb, tk_r, 21)
    both = added(nb, tk_s[b], tk_r)
    sc[b] = nn(both[:, :QR] * both[:, QR:], pick, HIGHEST)
    spread(nb, bdev, sc, b, 22)
    arrived(nb, sc, 22)
    every = sc[...].reshape(tokens, 128)
    scores_o[...] = every[:, :QUERIES]
    dc_s[...] = tn(every, member, HIGHEST)[0:8, :]
    to_mate(dc_s, dc_p, 23)
    wait_bytes(dc_p, recvs.at[23])
    dc_z[...] = dc_s[...] + dc_p[...]
    for k in near_first(nz):
        put(dc_z, dc_r.at[k], sends.at[24], recvs.at[24], zdev(k))
    sent.append((dc_r.at[pl.ds(0, nz - 1)], sends.at[24]))
    arrived(nz, dc_r, 24)
    docs = added(nz, dc_z[...], dc_r)
    full = jnp.concatenate([docs, jnp.zeros((120, docs.shape[1]), F32)], axis=0)
    doc_o[...] = full.T[:, :QUERIES]
    for ref, sem in sent:
        wait_bytes(ref, sem)


def local(nb, nz, eig_in, eig_out, eigvals, out_factors, in_factors, test_matrix, activations, gradients, doc_lengths):
    ra, cj = eig_in.shape
    ri, ca = eig_out.shape
    tokens = activations.shape[0]
    docs = doc_lengths.shape[0]
    nd = 2 * nz
    vm = pltpu.VMEM
    scratch = [
        vm((ra, cj), BF16),
        vm((ri, ca), BF16),
        vm((ri, cj), BF16),
        vm(out_factors.shape, BF16),
        vm(test_matrix.shape, BF16),
        vm(activations.shape, BF16),
        vm(gradients.shape, BF16),
        vm((1, docs), jnp.int32),
        vm((nd, ra // nd, QC), BF16),
        vm((QC, cj), F32),
        vm((ri, cj), F32),
        vm((QUERIES, cj, QR), BF16),
        vm((QUERIES, ri, cj), BF16),
        vm((nb, QC // nb, cj), BF16),
        vm((nb, QC // nb, cj), BF16),
        vm((nb, QC // nb, cj), BF16),
        vm((nd, ri // nd, QC), BF16),
        vm((nz, ri // nd, QC), BF16),
        vm((nz, ri // nd, QC), BF16),
        vm((nz, ri // nd, QC), BF16),
        vm((nd, ri // nd, QC), BF16),
        vm((nd, ri // nd, QR), BF16),
        vm((nz, ri // nd, QR), BF16),
        vm((nz, ri // nd, QR), BF16),
        vm((nz, ri // nd, QR), BF16),
        vm((nd, ri // nd, QR), BF16),
        vm((RANK, QR), F32),
        vm((nb, RANK, QR), F32),
        vm((nb, QR // nb, cj), BF16),
        vm((nb, QR // nb, cj), BF16),
        vm((nb, QR // nb, cj), BF16),
        vm((nb, ca // nb, QR), BF16),
        vm((nb, ca // nb, QR), BF16),
        vm((ca // nb, QR), BF16),
        vm((nd, ca // nb, QR), BF16),
        vm((nd, ra // nd, QR), BF16),
        vm((nz, ra // nd, QR), BF16),
        vm((nz, ra // nd, QR), BF16),
        vm((nz, ra // nd, QR), BF16),
        vm((nd, ra // nd, QR), BF16),
        vm((nb, tokens // nb, 2 * QR), F32),
        vm((nb, tokens // nb, 2 * QR), F32),
        vm((nb, tokens // nb, 128), F32),
        vm((8, docs), F32),
        vm((8, docs), F32),
        vm((8, docs), F32),
        vm((nz, 8, docs), F32),
        pltpu.SemaphoreType.DMA((9,)),
        pltpu.SemaphoreType.DMA(()),
        pltpu.SemaphoreType.DMA((nz,)),
        pltpu.SemaphoreType.DMA(()),
        pltpu.SemaphoreType.DMA((nz,)),
        pltpu.SemaphoreType.DMA((25,)),
        pltpu.SemaphoreType.DMA((25,)),
    ]
    return pl.pallas_call(
        functools.partial(body, nb, nz),
        out_shape=(
            jax.ShapeDtypeStruct((tokens, QUERIES), F32),
            jax.ShapeDtypeStruct((docs, QUERIES), F32),
        ),
        in_specs=[pl.BlockSpec(memory_space=pl.ANY)] * 9,
        out_specs=(pl.BlockSpec(memory_space=pltpu.VMEM), pl.BlockSpec(memory_space=pltpu.VMEM)),
        scratch_shapes=scratch,
        compiler_params=pltpu.CompilerParams(
            collective_id=0, has_side_effects=True, vmem_limit_bytes=60 * 1024 * 1024
        ),
        name="influence",
    )(
        eig_in,
        eig_out,
        eigvals,
        out_factors,
        in_factors,
        test_matrix,
        activations,
        gradients,
        doc_lengths.reshape(1, docs),
    )


def solution(mesh):
    nb = mesh.shape["basis"]
    nz = mesh.shape["docs"] // 2
    return jax.shard_map(
        functools.partial(local, nb, nz),
        mesh=mesh,
        in_specs=(
            P("basis", "docs"),
            P("basis", "docs"),
            P("basis", "docs"),
            P("docs", None),
            P(("basis", "docs"), None),
            P("docs", None),
            P("docs", "basis"),
            P("docs", "basis"),
            P(),
        ),
        out_specs=(P("docs", None), P()),
        check_vma=False,
    )
```

```python
import functools

import jax
import jax.numpy as jnp
from jax import lax
from jax.experimental import pallas as pl
from jax.experimental.pallas import tpu as pltpu
from jax.sharding import PartitionSpec as P

QUERIES = 4
LQ = 64
RANK = 32
QR = QUERIES * RANK
QC = QUERIES * LQ
DAMPING = 0.1
MESH = pl.DeviceIdType.MESH
HIGHEST = lax.Precision.HIGHEST
F32 = jnp.float32
BF16 = jnp.bfloat16


def nn(a, b, precision=None):
    return lax.dot_general(a, b, (((1,), (0,)), ((), ())), precision=precision, preferred_element_type=F32)


def nt(a, b, precision=None):
    return lax.dot_general(a, b, (((1,), (1,)), ((), ())), precision=precision, preferred_element_type=F32)


def tn(a, b, precision=None):
    return lax.dot_general(a, b, (((0,), (0,)), ((), ())), precision=precision, preferred_element_type=F32)


def iota(shape, axis):
    return lax.broadcasted_iota(jnp.int32, shape, axis)


def near_first(n):
    order = []
    for k in range(1, n // 2 + 1):
        order.append(k)
        if n - k != k:
            order.append(n - k)
    return order


def tree(n):
    if n == 16:
        return (6, -6, 3, -3), ((6, 2),)
    if n == 4:
        return (), ((0, 2),)
    return (), ()


def wait_bytes(ref, sem):
    pltpu.make_async_copy(ref, ref, sem).wait()


def body(
    nb,
    nz,
    ein_h,
    eout_h,
    lam_h,
    of_h,
    inf_h,
    te_h,
    act_h,
    gr_h,
    len_h,
    scores_o,
    doc_o,
    ein,
    eout,
    lam,
    outf,
    te,
    act,
    gr,
    lens,
    xin,
    acc,
    wgt,
    tsel,
    mom,
    pin_s,
    pin_r,
    rin,
    po_s,
    po_p,
    po_z,
    po_r,
    ro,
    sk_s,
    sk_p,
    sk_z,
    sk_r,
    sk,
    gm_s,
    gm_r,
    pj_s,
    pj_r,
    pj,
    lf_s,
    lf_r,
    lf_c,
    lf,
    rt_s,
    rt_p,
    rt_z,
    rt_l,
    rt_a,
    rt_r,
    rt,
    tk_s,
    tk_r,
    sc,
    dc_s,
    dc_p,
    dc_z,
    dc_r,
    in_sem,
    a_send,
    a_recv,
    f_send,
    f_recv,
    l_send,
    l_recv,
    j_send,
    j_recv,
    g_recv,
    sends,
    recvs,
):
    b = lax.axis_index("basis")
    d = lax.axis_index("docs")
    z = lax.div(d, 2)
    c = lax.rem(d, 2)
    mate = {"docs": z * 2 + (1 - c)}
    sent = []

    def zdev(k):
        return {"docs": lax.rem(z + k + nz, nz) * 2 + c}

    def bdev(k):
        return {"basis": lax.rem(b + k, nb)}

    def put(src, dst, s, r, dev):
        pltpu.make_async_remote_copy(
            src_ref=src, dst_ref=dst, send_sem=s, recv_sem=r, device_id=dev, device_id_type=MESH
        ).start()

    def to_mate(src, dst, ch):
        put(src, dst, sends.at[ch], recvs.at[ch], mate)
        sent.append((src, sends.at[ch]))

    def scatter(n, dev, me, src, base, dst, ch):
        for k in near_first(n):
            put(
                src.at[base + lax.rem(me + k, n)],
                dst.at[k],
                sends.at[ch],
                recvs.at[ch],
                dev(k),
            )
        sent.append((dst.at[pl.ds(0, n - 1)], sends.at[ch]))

    def spread(n, dev, ref, where, ch):
        for k in near_first(n):
            put(ref.at[where], ref.at[where], sends.at[ch], recvs.at[ch], dev(k))
        sent.append((ref.at[pl.ds(0, n - 1)], sends.at[ch]))

    def arrived(n, ref, ch):
        wait_bytes(ref.at[pl.ds(0, n - 1)], recvs.at[ch])

    def added(n, first, ref):
        total = first.astype(F32)
        for k in range(1, n):
            total = total + ref[k].astype(F32)
        return total

    loads = []
    for i, (src, dst) in enumerate(
        (
            (inf_h, xin.at[d]),
            (eout_h, eout),
            (of_h, outf),
            (ein_h, ein),
            (lam_h, lam),
            (te_h, te),
            (act_h, act),
            (gr_h, gr),
            (len_h, lens),
        )
    ):
        cp = pltpu.make_async_copy(src, dst, in_sem.at[i])
        cp.start()
        loads.append(cp)

    barrier = pltpu.get_barrier_semaphore()
    for k in near_first(nz):
        pl.semaphore_signal(barrier, inc=1, device_id=zdev(k), device_id_type=MESH)
    for k in near_first(nb):
        pl.semaphore_signal(barrier, inc=1, device_id=bdev(k), device_id_type=MESH)
    pl.semaphore_signal(barrier, inc=1, device_id=mate, device_id_type=MESH)
    twin = {"basis": z, "docs": b * 2 + c}

    @pl.when(b != z)
    def _():
        pl.semaphore_signal(barrier, inc=1, device_id=twin, device_id_type=MESH)

    pl.semaphore_wait(barrier, nz + nb - 1 + jnp.where(b != z, 1, 0))

    jumps, extra = tree(nz)
    near = (1, -1) if nz > 2 else (1,)
    beyond = dict(extra)

    def forward(slot, off, s, r):
        for step in near + ((beyond[off],) if off in beyond else ()):
            put(slot(off), slot(off), s, r(off + step), zdev(step))

    def tree_gather(slot, s, r):
        for j in jumps:
            put(slot(0), slot(0), s, r(j), zdev(j))
        forward(slot, 0, s, r)

    def slot_in(off):
        return xin.at[lax.rem(z - off + nz, nz) * 2 + c]

    def slot_of(ref):
        return lambda off: ref.at[c * nz + lax.rem(z - off + nz, nz)]

    centers = jumps + (0,)

    def leaves(parts, ref, s, r):
        count = 0
        for i, e in enumerate(centers):
            steps = near + ((beyond[e],) if e in beyond else ())
            for m, step in enumerate(steps):
                target = lax.rem(z - e - step + 2 * nz, nz)
                put(parts.at[target], ref.at[3 * i + m], s, r.at[i], zdev(-step))
                count += 1
        sent.append((parts.at[pl.ds(0, count)], s))

    def roots(parts, ref, agg, got, r, js, jr):
        total = None
        for i, e in enumerate(centers):
            steps = near + ((beyond[e],) if e in beyond else ())
            wait_bytes(ref.at[pl.ds(3 * i, len(steps))], r.at[i])
            total = parts[lax.rem(z - e + nz, nz)].astype(F32)
            for m in range(len(steps)):
                total = total + ref[3 * i + m].astype(F32)
            if e != 0:
                agg[i] = total.astype(BF16)
                put(agg.at[i], got.at[i], js, jr, zdev(-e))
        if len(jumps) > 0:
            sent.append((agg.at[pl.ds(0, len(jumps))], js))
            wait_bytes(got.at[pl.ds(0, len(jumps))], jr)
            for i in range(len(jumps)):
                total = total + got[i].astype(F32)
        return total

    order = list(near) + ([beyond[0]] if 0 in beyond else [])
    for j in sorted(jumps, key=abs):
        order.append(j)
    for j in sorted(jumps, key=abs):
        order += [j + e for e in near] + ([j + beyond[j]] if j in beyond else [])
    loads[0].wait()
    tree_gather(slot_in, a_send, lambda off: a_recv.at[off % nz])
    sent.append((xin.at[pl.ds(0, nz - 1)], a_send))
    put(xin.at[d], xin.at[d], f_send, f_recv.at[0], mate)

    loads[1].wait()
    loads[2].wait()
    part = nn(eout[...], outf[...])
    po_s[...] = part.astype(BF16).reshape(po_s.shape)
    to_mate(po_s.at[pl.ds((1 - c) * nz, nz)], po_p, 0)

    loads[4].wait()
    wgt[...] = 1.0 / (lam[...].astype(F32) + DAMPING)
    loads[5].wait()
    wide = jnp.concatenate([te[...].astype(F32)] * QUERIES, axis=0).T
    for q in range(QUERIES):
        tsel[q] = jnp.where(lax.div(iota(wide.shape, 1), RANK) == q, wide, 0.0).astype(BF16)

    wait_bytes(po_p, recvs.at[0])
    po_z[...] = (po_s[pl.ds(c * nz, nz)].astype(F32) + po_p[...].astype(F32)).astype(BF16)

    scatter(nz, zdev, z, po_z, 0, po_r, 1)

    for off in order:
        pltpu.make_async_copy(slot_in(off), slot_in(off), a_recv.at[off % nz]).wait()
        if off in jumps:
            forward(slot_in, off, a_send, lambda o: a_recv.at[o % nz])
        put(slot_in(off), slot_in(off), f_send, f_recv.at[off % nz], mate)
    sent.append((xin.at[pl.ds(0, nz)], f_send))
    arrived(nz, po_r, 1)
    ro[c * nz + z] = added(nz, po_z[z], po_r).astype(BF16)
    spread(nz, zdev, ro, c * nz + z, 3)
    for k in range(nz):
        other = lax.rem(z - k + nz, nz) * 2 + 1 - c
        pltpu.make_async_copy(xin.at[other], xin.at[other], f_recv.at[k]).wait()

    loads[3].wait()
    pieces = xin.shape[0] // 4
    rows = pieces * xin.shape[1]
    for i in range(4):
        x = xin[pl.ds(i * pieces, pieces)].astype(F32).reshape(rows, QC).astype(BF16)
        t = tn(x, ein[pl.ds(i * rows, rows), :])
        if i == 0:
            acc[...] = t
        elif i < 3:
            acc[...] += t
        else:
            t = acc[...] + t
            pin_s[...] = t.astype(BF16).reshape(pin_s.shape)
    scatter(nb, bdev, b, pin_s, 0, pin_r, 2)

    arrived(nb, pin_r, 2)
    rin[b] = added(nb, pin_s[b], pin_r).astype(BF16)
    spread(nb, bdev, rin, b, 4)

    arrived(nz, ro, 3)
    to_mate(ro.at[pl.ds(c * nz, nz)], ro.at[pl.ds(c * nz, nz)], 5)
    wait_bytes(ro.at[pl.ds(0, nz)], recvs.at[5])
    arrived(nb, rin, 4)

    rows_out = eout.shape[0]
    cols_in = ein.shape[1]
    rotin = rin[...].reshape(QC, cols_in)
    step = 128
    per = sk_s.shape[1]
    per_block = step // per
    blocks = nz // per_block
    for h in range(2):
        side = 1 - c if h == 0 else c
        for i in range(blocks):
            slot = side * nz + i * per_block
            at = pl.multiple_of(slot * per, step)
            block = ro[pl.ds(slot, per_block)].reshape(step, QC).astype(F32)
            lane = lax.div(iota(block.shape, 1), LQ)
            total = None
            for q in range(QUERIES):
                only = jnp.where(lane == q, block, 0.0).astype(BF16)
                m = (nn(only, rotin) * wgt[pl.ds(at, step), :]).astype(BF16)
                mom[q, pl.ds(at, step), :] = m
                t = nn(m, tsel[q])
                total = t if total is None else total + t
            sk_s[pl.ds(slot, per_block)] = total.astype(BF16).reshape(per_block, per, QR)
        if h == 0:
            to_mate(sk_s.at[pl.ds((1 - c) * nz, nz)], sk_p, 6)
    wait_bytes(sk_p, recvs.at[6])
    sk_z[...] = (sk_s[pl.ds(c * nz, nz)].astype(F32) + sk_p[...].astype(F32)).astype(BF16)
    scatter(nz, zdev, z, sk_z, 0, sk_r, 7)
    arrived(nz, sk_r, 7)
    sk[c * nz + z] = added(nz, sk_z[z], sk_r).astype(BF16)
    spread(nz, zdev, sk, c * nz + z, 8)
    arrived(nz, sk, 8)
    to_mate(sk.at[pl.ds(c * nz, nz)], sk.at[pl.ds(c * nz, nz)], 9)
    wait_bytes(sk.at[pl.ds(0, nz)], recvs.at[9])

    sketch = sk[...].reshape(rows_out, QR).astype(F32).T.astype(BF16)
    gram = nt(sketch, sketch)
    lane_q = lax.div(iota((RANK, QR), 1), RANK)
    mine = jnp.zeros((RANK, QR), F32)
    for q in range(QUERIES):
        mine = mine + jnp.where(lane_q == q, gram[q * RANK : (q + 1) * RANK, :], 0.0)
    gm_s[...] = mine
    for k in near_first(nb):
        put(gm_s, gm_r.at[k], sends.at[10], recvs.at[10], bdev(k))
    sent.append((gm_r.at[pl.ds(0, nb - 1)], sends.at[10]))

    raw = jnp.concatenate(
        [nn(sketch[q * RANK : (q + 1) * RANK, :], mom[q]) for q in range(QUERIES)], axis=0
    )
    acc[pl.ds(0, QR), :] = raw
    left_raw = nn(sketch, eout[...])

    arrived(nb, gm_r, 10)
    a0 = added(nb, mine, gm_r)
    row = iota((RANK, QR), 0)
    lane = iota((RANK, QR), 1)
    in_q = lane - lane_q * RANK

    def over_lanes(x):
        out = jnp.zeros((RANK, QR), F32)
        for q in range(QUERIES):
            s = jnp.sum(jnp.where(lane_q == q, x, 0.0), axis=1, keepdims=True)
            out = jnp.where(lane_q == q, s, out)
        return out

    def eliminate(k, carry):
        a, e = carry
        col = over_lanes(jnp.where(in_q == k, a, 0.0))
        at = row == k
        pivot = jnp.sum(jnp.where(at, col, 0.0), axis=0, keepdims=True)
        row_a = jnp.sum(jnp.where(at, a, 0.0), axis=0, keepdims=True)
        row_e = jnp.sum(jnp.where(at, e, 0.0), axis=0, keepdims=True)
        f = jnp.where(row > k, col / pivot, 0.0)
        return a - f * row_a, e - f * row_e

    e0 = jnp.where(in_q == row, 1.0, 0.0).astype(F32)
    a1, e1 = lax.fori_loop(0, RANK, eliminate, (a0, e0))
    inv = e1 / jnp.sqrt(over_lanes(jnp.where(in_q == row, a1, 0.0)))
    tall = jnp.concatenate([inv] * QUERIES, axis=0)
    same = lax.div(iota((QR, QR), 0), RANK) == lax.div(iota((QR, QR), 1), RANK)
    solve = jnp.where(same, tall, 0.0)

    pj_s[...] = nn(solve, acc[pl.ds(0, QR), :], HIGHEST).reshape(pj_s.shape).astype(BF16)
    scatter(nb, bdev, b, pj_s, 0, pj_r, 11)
    lf_s[...] = nn(solve, left_raw, HIGHEST).T.reshape(lf_s.shape).astype(BF16)
    scatter(nb, bdev, b, lf_s, 0, lf_r, 12)
    arrived(nb, pj_r, 11)
    pj[b] = added(nb, pj_s[b], pj_r).astype(BF16)
    spread(nb, bdev, pj, b, 13)
    arrived(nb, lf_r, 12)
    left_here = added(nb, lf_s[b], lf_r).astype(BF16)
    lf_c[...] = left_here

    @pl.when(b == z)
    def _():
        lf[c * nz + z] = left_here

    @pl.when(b != z)
    def _():
        put(lf_c, lf.at[c * nz + b], sends.at[14], recvs.at[14], twin)

    arrived(nb, pj, 13)
    proj = pj[...].astype(F32).reshape(QR, cols_in).astype(BF16)

    slots = nz // 2
    tall_rows = slots * rt_s.shape[1]
    for h in range(4):
        slot = (1 - c if h < 2 else c) * nz + (h % 2) * slots
        at = pl.multiple_of(slot * rt_s.shape[1], tall_rows)
        r = nt(ein[pl.ds(at, tall_rows), :], proj)
        rt_s[pl.ds(slot, slots)] = r.reshape(slots, rt_s.shape[1], QR).astype(BF16)
        if h == 1:
            to_mate(rt_s.at[pl.ds((1 - c) * nz, nz)], rt_p, 15)
    wait_bytes(rt_p, recvs.at[15])
    rt_z[...] = (rt_s[pl.ds(c * nz, nz)].astype(F32) + rt_p[...].astype(F32)).astype(BF16)
    leaves(rt_z, rt_l, l_send, l_recv)

    @pl.when(b != z)
    def _():
        wait_bytes(lf_c, recvs.at[14])
        wait_bytes(lf_c, sends.at[14])

    spread(nz, zdev, lf, c * nz + z, 17)
    rt[c * nz + z] = roots(rt_z, rt_l, rt_a, rt_r, l_recv, j_send, j_recv).astype(BF16)
    slot_rt = slot_of(rt)
    tree_gather(slot_rt, sends.at[18], lambda off: g_recv.at[jumps.index(off)] if off in jumps else recvs.at[18])
    arrived(nz, lf, 17)
    to_mate(lf.at[pl.ds(c * nz, nz)], lf.at[pl.ds(c * nz, nz)], 19)
    for j in jumps:
        wait_bytes(slot_rt(j), g_recv.at[jumps.index(j)])
        forward(slot_rt, j, sends.at[18], lambda off: recvs.at[18])
    wait_bytes(rt.at[pl.ds(0, nz - 1 - len(jumps))], recvs.at[18])
    sent.append((rt.at[pl.ds(0, nz - 1)], sends.at[18]))
    to_mate(rt.at[pl.ds(c * nz, nz)], rt.at[pl.ds(c * nz, nz)], 20)

    loads[6].wait()
    loads[7].wait()
    loads[8].wait()
    wait_bytes(lf.at[pl.ds(0, nz)], recvs.at[19])
    left = lf[...].astype(F32).reshape(gr.shape[1], QR).astype(BF16)
    tk_s[:, :, QR:] = nn(gr[...], left).reshape(nb, -1, QR)
    half = act.shape[1] // 2
    tokens = act.shape[0]
    wait_bytes(rt.at[pl.ds(0, nz)], recvs.at[20])
    tok = None
    for i in range(2):
        right = rt[pl.ds(i * nz, nz)].astype(F32).reshape(half, QR).astype(BF16)
        t = nn(act[:, i * half : (i + 1) * half], right)
        tok = t if tok is None else tok + t
    tk_s[:, :, :QR] = tok.reshape(nb, -1, QR)
    scatter(nb, bdev, b, tk_s, 0, tk_r, 21)

    here = d * tokens + iota((tokens, lens.shape[1]), 0)
    length = lens[...].astype(F32)
    earlier = jnp.where(
        iota((lens.shape[1],) * 2, 0) < iota((lens.shape[1],) * 2, 1), 1.0, 0.0
    ).astype(BF16)
    start = nn(jnp.broadcast_to(length, (8, lens.shape[1])).astype(BF16), earlier)[0:1, :]
    stop = start + length
    place = here.astype(F32)
    member = jnp.where((place >= start) & (place < stop), 1.0, 0.0).astype(F32)
    pick = jnp.where(
        lax.div(iota((QR, 128), 0), RANK) == iota((QR, 128), 1), 1.0, 0.0
    ).astype(F32)

    arrived(nb, tk_r, 21)
    both = added(nb, tk_s[b], tk_r)
    sc[b] = nn(both[:, :QR] * both[:, QR:], pick, HIGHEST)
    spread(nb, bdev, sc, b, 22)
    arrived(nb, sc, 22)
    every = sc[...].reshape(tokens, 128)
    scores_o[...] = every.T[:QUERIES, :]
    dc_s[...] = tn(every, member, HIGHEST)[0:QUERIES, :]
    to_mate(dc_s, dc_p, 23)
    wait_bytes(dc_p, recvs.at[23])
    dc_z[...] = dc_s[...] + dc_p[...]
    for k in near_first(nz):
        put(dc_z, dc_r.at[k], sends.at[24], recvs.at[24], zdev(k))
    sent.append((dc_r.at[pl.ds(0, nz - 1)], sends.at[24]))
    arrived(nz, dc_r, 24)
    docs = added(nz, dc_z[...], dc_r)
    doc_o[...] = docs
    for ref, sem in sent:
        wait_bytes(ref, sem)


def local(nb, nz, eig_in, eig_out, eigvals, out_factors, in_factors, test_matrix, activations, gradients, doc_lengths):
    ra, cj = eig_in.shape
    ri, ca = eig_out.shape
    tokens = activations.shape[0]
    docs = doc_lengths.shape[0]
    nd = 2 * nz
    vm = pltpu.VMEM
    scratch = [
        vm((ra, cj), BF16),
        vm((ri, ca), BF16),
        vm((ri, cj), BF16),
        vm(out_factors.shape, BF16),
        vm((RANK, cj), BF16),
        vm(activations.shape, BF16),
        vm(gradients.shape, BF16),
        vm((1, docs), jnp.int32),
        vm((nd, ra // nd, QC), BF16),
        vm((QC, cj), F32),
        vm((ri, cj), F32),
        vm((QUERIES, cj, QR), BF16),
        vm((QUERIES, ri, cj), BF16),
        vm((nb, QC // nb, cj), BF16),
        vm((nb, QC // nb, cj), BF16),
        vm((nb, QC // nb, cj), BF16),
        vm((nd, ri // nd, QC), BF16),
        vm((nz, ri // nd, QC), BF16),
        vm((nz, ri // nd, QC), BF16),
        vm((nz, ri // nd, QC), BF16),
        vm((nd, ri // nd, QC), BF16),
        vm((nd, ri // nd, QR), BF16),
        vm((nz, ri // nd, QR), BF16),
        vm((nz, ri // nd, QR), BF16),
        vm((nz, ri // nd, QR), BF16),
        vm((nd, ri // nd, QR), BF16),
        vm((RANK, QR), F32),
        vm((nb, RANK, QR), F32),
        vm((nb, QR // nb, cj), BF16),
        vm((nb, QR // nb, cj), BF16),
        vm((nb, QR // nb, cj), BF16),
        vm((nb, ca // nb, QR), BF16),
        vm((nb, ca // nb, QR), BF16),
        vm((ca // nb, QR), BF16),
        vm((nd, ca // nb, QR), BF16),
        vm((nd, ra // nd, QR), BF16),
        vm((nz, ra // nd, QR), BF16),
        vm((nz, ra // nd, QR), BF16),
        vm((15, ra // nd, QR), BF16),
        vm((4, ra // nd, QR), BF16),
        vm((4, ra // nd, QR), BF16),
        vm((nd, ra // nd, QR), BF16),
        vm((nb, tokens // nb, 2 * QR), F32),
        vm((nb, tokens // nb, 2 * QR), F32),
        vm((nb, tokens // nb, 128), F32),
        vm((QUERIES, docs), F32),
        vm((QUERIES, docs), F32),
        vm((QUERIES, docs), F32),
        vm((nz, QUERIES, docs), F32),
        pltpu.SemaphoreType.DMA((9,)),
        pltpu.SemaphoreType.DMA(()),
        pltpu.SemaphoreType.DMA((nz,)),
        pltpu.SemaphoreType.DMA(()),
        pltpu.SemaphoreType.DMA((nz,)),
        pltpu.SemaphoreType.DMA(()),
        pltpu.SemaphoreType.DMA((5,)),
        pltpu.SemaphoreType.DMA(()),
        pltpu.SemaphoreType.DMA(()),
        pltpu.SemaphoreType.DMA((4,)),
        pltpu.SemaphoreType.DMA((25,)),
        pltpu.SemaphoreType.DMA((25,)),
    ]
    scores, influence = pl.pallas_call(
        functools.partial(body, nb, nz),
        out_shape=(
            jax.ShapeDtypeStruct((QUERIES, tokens), F32),
            jax.ShapeDtypeStruct((QUERIES, docs), F32),
        ),
        in_specs=[pl.BlockSpec(memory_space=pl.ANY)] * 9,
        out_specs=(pl.BlockSpec(memory_space=pltpu.VMEM), pl.BlockSpec(memory_space=pltpu.VMEM)),
        scratch_shapes=scratch,
        compiler_params=pltpu.CompilerParams(
            collective_id=0, has_side_effects=True, vmem_limit_bytes=60 * 1024 * 1024
        ),
        name="influence",
    )(
        eig_in,
        eig_out,
        eigvals,
        out_factors,
        in_factors,
        test_matrix.T,
        activations,
        gradients,
        doc_lengths.reshape(1, docs),
    )
    def leave(a, b, x, y):
        x[...] = a[...]
        y[...] = b[...]

    scores, influence = pl.pallas_call(
        leave,
        out_shape=(
            jax.ShapeDtypeStruct(scores.shape, F32),
            jax.ShapeDtypeStruct(influence.shape, F32),
        ),
        name="leave",
    )(scores, influence)
    return scores.T, influence.T


def solution(mesh):
    nb = mesh.shape["basis"]
    nz = mesh.shape["docs"] // 2
    return jax.shard_map(
        functools.partial(local, nb, nz),
        mesh=mesh,
        in_specs=(
            P("basis", "docs"),
            P("basis", "docs"),
            P("basis", "docs"),
            P("docs", None),
            P(("basis", "docs"), None),
            P("docs", None),
            P("docs", "basis"),
            P("docs", "basis"),
            P(),
        ),
        out_specs=(P("docs", None), P()),
        check_vma=False,
    )
```

```python
import functools

import jax
import jax.numpy as jnp
from jax import lax
from jax.experimental import pallas as pl
from jax.experimental.pallas import tpu as pltpu
from jax.sharding import PartitionSpec as P

QUERIES = 4
LQ = 64
RANK = 32
QR = QUERIES * RANK
QC = QUERIES * LQ
DAMPING = 0.1
MESH = pl.DeviceIdType.MESH
HIGHEST = lax.Precision.HIGHEST
F32 = jnp.float32
BF16 = jnp.bfloat16


def nn(a, b, precision=None):
    return lax.dot_general(a, b, (((1,), (0,)), ((), ())), precision=precision, preferred_element_type=F32)


def nt(a, b, precision=None):
    return lax.dot_general(a, b, (((1,), (1,)), ((), ())), precision=precision, preferred_element_type=F32)


def tn(a, b, precision=None):
    return lax.dot_general(a, b, (((0,), (0,)), ((), ())), precision=precision, preferred_element_type=F32)


def iota(shape, axis):
    return lax.broadcasted_iota(jnp.int32, shape, axis)


def ring(k, n):
    return min(k, n - k)


def far_first(n):
    return sorted(range(1, n), key=lambda k: -ring(k, n))


def far_first_grid(n, side):
    if side == 1:
        return far_first(n)
    return sorted(range(1, n), key=lambda k: -ring(k // side, side) - ring(k % side, side))


def tree(n):
    if n == 16:
        return (6, -6, 3, -3), ((6, 2),)
    if n == 4:
        return (), ((0, 2),)
    return (), ()


def wait_bytes(ref, sem):
    pltpu.make_async_copy(ref, ref, sem).wait()


def body(
    nb,
    nz,
    ein_h,
    eout_h,
    lam_h,
    of_h,
    inf_h,
    te_h,
    act_h,
    gr_h,
    len_h,
    scores_o,
    doc_o,
    ein,
    eout,
    lam,
    outf,
    te,
    act,
    gr,
    lens,
    xin,
    acc,
    wgt,
    tsel,
    mom,
    pin_s,
    pin_r,
    rin,
    po_s,
    po_p,
    po_z,
    po_l,
    po_a,
    po_r,
    ro,
    sk_s,
    sk_p,
    sk_z,
    sk_r,
    sk,
    gm_s,
    gm_r,
    pj_s,
    pj_r,
    pj,
    lf_s,
    lf_r,
    lf_c,
    lf,
    rt_s,
    rt_p,
    rt_z,
    rt_l,
    rt_a,
    rt_r,
    rt,
    tk_s,
    tk_r,
    sc,
    dc_s,
    dc_p,
    dc_z,
    dc_r,
    in_sem,
    a_send,
    a_recv,
    f_send,
    f_recv,
    l_send,
    l_recv,
    j_send,
    j_recv,
    g_recv,
    p_send,
    p_recv,
    q_send,
    q_recv,
    h_recv,
    sends,
    recvs,
):
    b = lax.axis_index("basis")
    d = lax.axis_index("docs")
    z = lax.div(d, 2)
    c = lax.rem(d, 2)
    mate = {"docs": z * 2 + (1 - c)}
    sent = []

    def zdev(k):
        return {"docs": lax.rem(z + k + nz, nz) * 2 + c}

    side = 4 if nb == 16 else 2 if nb == 4 else 1

    def bpeer(k):
        if side == 1:
            return lax.rem(b + k, nb)
        across = lax.rem(lax.div(b, side) + k // side, side)
        return across * side + lax.rem(lax.rem(b, side) + k % side, side)

    def zpeer(k):
        return lax.rem(z + k, nz)

    def bdev(k):
        return {"basis": bpeer(k)}

    zfar, bfar = far_first(nz), far_first_grid(nb, side)

    def put(src, dst, s, r, dev):
        pltpu.make_async_remote_copy(
            src_ref=src, dst_ref=dst, send_sem=s, recv_sem=r, device_id=dev, device_id_type=MESH
        ).start()

    def to_mate(src, dst, ch):
        put(src, dst, sends.at[ch], recvs.at[ch], mate)
        sent.append((src, sends.at[ch]))

    def scatter(n, peer, dev, far, src, dst, ch):
        for k in far:
            put(
                src.at[peer(k)],
                dst.at[k],
                sends.at[ch],
                recvs.at[ch],
                dev(k),
            )
        sent.append((dst.at[pl.ds(0, n - 1)], sends.at[ch]))

    def spread(n, dev, far, ref, where, ch):
        for k in far:
            put(ref.at[where], ref.at[where], sends.at[ch], recvs.at[ch], dev(k))
        sent.append((ref.at[pl.ds(0, n - 1)], sends.at[ch]))

    def arrived(n, ref, ch):
        wait_bytes(ref.at[pl.ds(0, n - 1)], recvs.at[ch])

    def added(n, first, ref):
        total = first.astype(F32)
        for k in range(1, n):
            total = total + ref[k].astype(F32)
        return total

    loads = []
    for i, (src, dst) in enumerate(
        (
            (inf_h, xin.at[d]),
            (eout_h, eout),
            (of_h, outf),
            (ein_h, ein),
            (lam_h, lam),
            (te_h, te),
            (act_h, act),
            (gr_h, gr),
            (len_h, lens),
        )
    ):
        cp = pltpu.make_async_copy(src, dst, in_sem.at[i])
        cp.start()
        loads.append(cp)

    barrier = pltpu.get_barrier_semaphore()
    for k in zfar:
        pl.semaphore_signal(barrier, inc=1, device_id=zdev(k), device_id_type=MESH)
    for k in bfar:
        pl.semaphore_signal(barrier, inc=1, device_id=bdev(k), device_id_type=MESH)
    pl.semaphore_signal(barrier, inc=1, device_id=mate, device_id_type=MESH)
    twin = {"basis": z, "docs": b * 2 + c}

    @pl.when(b != z)
    def _():
        pl.semaphore_signal(barrier, inc=1, device_id=twin, device_id_type=MESH)

    pl.semaphore_wait(barrier, nz + nb - 1 + jnp.where(b != z, 1, 0))

    jumps, extra = tree(nz)
    near = (1, -1) if nz > 2 else (1,)
    beyond = dict(extra)

    def forward(slot, off, s, r):
        for step in near + ((beyond[off],) if off in beyond else ()):
            put(slot(off), slot(off), s, r(off + step), zdev(step))

    def tree_gather(slot, s, r):
        for j in jumps:
            put(slot(0), slot(0), s, r(j), zdev(j))
        forward(slot, 0, s, r)

    def slot_in(off):
        return xin.at[lax.rem(z - off + nz, nz) * 2 + c]

    def slot_of(ref):
        return lambda off: ref.at[c * nz + lax.rem(z - off + nz, nz)]

    centers = jumps + (0,)

    def leaves(parts, ref, s, r):
        count = 0
        for i, e in enumerate(centers):
            steps = near + ((beyond[e],) if e in beyond else ())
            for m, step in enumerate(steps):
                target = lax.rem(z - e - step + 2 * nz, nz)
                put(parts.at[target], ref.at[3 * i + m], s, r.at[i], zdev(-step))
                count += 1
        sent.append((parts.at[pl.ds(0, count)], s))

    def gather_in(parts, ref, agg, got, r, js, jr):
        total = None
        for i, e in enumerate(centers):
            steps = near + ((beyond[e],) if e in beyond else ())
            wait_bytes(ref.at[pl.ds(3 * i, len(steps))], r.at[i])
            total = parts[lax.rem(z - e + nz, nz)].astype(F32)
            for m in range(len(steps)):
                total = total + ref[3 * i + m].astype(F32)
            if e != 0:
                agg[i] = total.astype(BF16)
                put(agg.at[i], got.at[i], js, jr, zdev(-e))
        if len(jumps) > 0:
            sent.append((agg.at[pl.ds(0, len(jumps))], js))
        return total

    def roots(total, got, jr):
        if len(jumps) > 0:
            wait_bytes(got.at[pl.ds(0, len(jumps))], jr)
            for i in range(len(jumps)):
                total = total + got[i].astype(F32)
        return total.astype(BF16)

    def relay(slot, ref, ch, rj):
        for j in sorted(jumps, key=abs):
            wait_bytes(slot(j), rj.at[jumps.index(j)])
            forward(slot, j, sends.at[ch], lambda off: recvs.at[ch])
        sent.append((ref.at[pl.ds(0, nz - 1)], sends.at[ch]))

    def launch(slot, ch, rj):
        tree_gather(slot, sends.at[ch], lambda off: rj.at[jumps.index(off)] if off in jumps else recvs.at[ch])

    def landed(ref, ch):
        wait_bytes(ref.at[pl.ds(0, nz - 1 - len(jumps))], recvs.at[ch])

    order = list(near) + ([beyond[0]] if 0 in beyond else [])
    for j in sorted(jumps, key=abs):
        order.append(j)
    for j in sorted(jumps, key=abs):
        order += [j + e for e in near] + ([j + beyond[j]] if j in beyond else [])
    loads[0].wait()
    tree_gather(slot_in, a_send, lambda off: a_recv.at[off % nz])
    sent.append((xin.at[pl.ds(0, nz - 1)], a_send))
    put(xin.at[d], xin.at[d], f_send, f_recv.at[0], mate)

    loads[1].wait()
    loads[2].wait()
    part = nn(eout[...], outf[...])
    po_s[...] = part.astype(BF16).reshape(po_s.shape)
    to_mate(po_s.at[pl.ds((1 - c) * nz, nz)], po_p, 0)

    loads[4].wait()
    wgt[...] = 1.0 / (lam[...].astype(F32) + DAMPING)
    loads[5].wait()
    wide = jnp.concatenate([te[...].astype(F32)] * QUERIES, axis=0).T
    for q in range(QUERIES):
        tsel[q] = jnp.where(lax.div(iota(wide.shape, 1), RANK) == q, wide, 0.0).astype(BF16)

    wait_bytes(po_p, recvs.at[0])
    po_z[...] = (po_s[pl.ds(c * nz, nz)].astype(F32) + po_p[...].astype(F32)).astype(BF16)

    leaves(po_z, po_l, p_send, p_recv)

    def take_in(off):
        pltpu.make_async_copy(slot_in(off), slot_in(off), a_recv.at[off % nz]).wait()
        if off in jumps:
            forward(slot_in, off, a_send, lambda o: a_recv.at[o % nz])
        put(slot_in(off), slot_in(off), f_send, f_recv.at[off % nz], mate)

    split = len(order) - sum(len(near) + (j in beyond) for j in jumps)
    for off in order[:split]:
        take_in(off)
    out_sum = gather_in(po_z, po_l, po_a, po_r, p_recv, q_send, q_recv)
    for off in order[split:]:
        take_in(off)
    sent.append((xin.at[pl.ds(0, nz)], f_send))
    for k in range(nz):
        other = lax.rem(z - k + nz, nz) * 2 + 1 - c
        pltpu.make_async_copy(xin.at[other], xin.at[other], f_recv.at[k]).wait()

    loads[3].wait()
    pieces = xin.shape[0] // 4
    rows = pieces * xin.shape[1]
    for i in range(4):
        x = xin[pl.ds(i * pieces, pieces)].astype(F32).reshape(rows, QC).astype(BF16)
        t = tn(x, ein[pl.ds(i * rows, rows), :])
        if i == 0:
            acc[...] = t
        elif i < 3:
            acc[...] += t
        else:
            t = acc[...] + t
            pin_s[...] = t.astype(BF16).reshape(pin_s.shape)
    scatter(nb, bpeer, bdev, bfar, pin_s, pin_r, 2)
    ro[c * nz + z] = roots(out_sum, po_r, q_recv)
    slot_ro = slot_of(ro)
    launch(slot_ro, 3, h_recv)

    arrived(nb, pin_r, 2)
    rin[b] = added(nb, pin_s[b], pin_r).astype(BF16)
    spread(nb, bdev, bfar, rin, b, 4)

    relay(slot_ro, ro, 3, h_recv)
    landed(ro, 3)
    to_mate(ro.at[pl.ds(c * nz, nz)], ro.at[pl.ds(c * nz, nz)], 5)
    wait_bytes(ro.at[pl.ds(0, nz)], recvs.at[5])
    arrived(nb, rin, 4)

    rows_out = eout.shape[0]
    cols_in = ein.shape[1]
    rotin = rin[...].reshape(QC, cols_in)
    step = 128
    per = sk_s.shape[1]
    per_block = step // per
    blocks = nz // per_block
    for h in range(2):
        who = 1 - c if h == 0 else c
        for i in range(blocks):
            slot = who * nz + i * per_block
            at = pl.multiple_of(slot * per, step)
            block = ro[pl.ds(slot, per_block)].reshape(step, QC).astype(F32)
            lane = lax.div(iota(block.shape, 1), LQ)
            total = None
            for q in range(QUERIES):
                only = jnp.where(lane == q, block, 0.0).astype(BF16)
                m = (nn(only, rotin) * wgt[pl.ds(at, step), :]).astype(BF16)
                mom[q, pl.ds(at, step), :] = m
                t = nn(m, tsel[q])
                total = t if total is None else total + t
            sk_s[pl.ds(slot, per_block)] = total.astype(BF16).reshape(per_block, per, QR)
        if h == 0:
            to_mate(sk_s.at[pl.ds((1 - c) * nz, nz)], sk_p, 6)
    wait_bytes(sk_p, recvs.at[6])
    sk_z[...] = (sk_s[pl.ds(c * nz, nz)].astype(F32) + sk_p[...].astype(F32)).astype(BF16)
    scatter(nz, zpeer, zdev, zfar, sk_z, sk_r, 7)
    arrived(nz, sk_r, 7)
    sk[c * nz + z] = added(nz, sk_z[z], sk_r).astype(BF16)
    spread(nz, zdev, zfar, sk, c * nz + z, 8)
    arrived(nz, sk, 8)
    to_mate(sk.at[pl.ds(c * nz, nz)], sk.at[pl.ds(c * nz, nz)], 9)
    wait_bytes(sk.at[pl.ds(0, nz)], recvs.at[9])

    sketch = sk[...].reshape(rows_out, QR).astype(F32).T.astype(BF16)
    gram = nt(sketch, sketch)
    lane_q = lax.div(iota((RANK, QR), 1), RANK)
    mine = jnp.zeros((RANK, QR), F32)
    for q in range(QUERIES):
        mine = mine + jnp.where(lane_q == q, gram[q * RANK : (q + 1) * RANK, :], 0.0)
    gm_s[...] = mine
    for k in bfar:
        put(gm_s, gm_r.at[k], sends.at[10], recvs.at[10], bdev(k))
    sent.append((gm_r.at[pl.ds(0, nb - 1)], sends.at[10]))

    raw = jnp.concatenate(
        [nn(sketch[q * RANK : (q + 1) * RANK, :], mom[q]) for q in range(QUERIES)], axis=0
    )
    acc[pl.ds(0, QR), :] = raw
    left_raw = nn(sketch, eout[...])

    arrived(nb, gm_r, 10)
    a0 = added(nb, mine, gm_r)
    group = 8
    spot = iota((group, QR), 0)
    lane_t = lax.div(iota((group, QR), 1), RANK)
    in_q = iota((group, QR), 1) - lane_t * RANK

    def over_lanes(x):
        out = None
        for q in range(QUERIES):
            s = jnp.sum(jnp.where(lane_t == q, x, 0.0), axis=1, keepdims=True)
            out = jnp.broadcast_to(s, x.shape) if out is None else jnp.where(lane_t == q, s, out)
        return out

    tiles = RANK // group
    a = [a0[t * group : (t + 1) * group, :] for t in range(tiles)]
    e = [jnp.where(in_q == spot + t * group, 1.0, 0.0).astype(F32) for t in range(tiles)]
    for k in range(RANK):
        first, at = k // group, k % group
        col = [over_lanes(jnp.where(in_q == k, a[t], 0.0)) for t in range(first, tiles)]
        pivot = 1.0 / col[0][at : at + 1, :]
        row_a = a[first][at : at + 1, :] * pivot
        row_e = e[first][at : at + 1, :] * pivot
        for t in range(first, tiles):
            f = col[t - first]
            if t == first:
                f = jnp.where(spot > at, f, 0.0)
            a[t] = a[t] - f * row_a
            e[t] = e[t] - f * row_e
    inv = jnp.concatenate(
        [
            e[t] / jnp.sqrt(over_lanes(jnp.where(in_q == spot + t * group, a[t], 0.0)))
            for t in range(tiles)
        ],
        axis=0,
    )
    tall = jnp.concatenate([inv] * QUERIES, axis=0)
    same = lax.div(iota((QR, QR), 0), RANK) == lax.div(iota((QR, QR), 1), RANK)
    solve = jnp.where(same, tall, 0.0)

    pj_s[...] = nn(solve, acc[pl.ds(0, QR), :], HIGHEST).reshape(pj_s.shape).astype(BF16)
    scatter(nb, bpeer, bdev, bfar, pj_s, pj_r, 11)
    lf_s[...] = nn(solve, left_raw, HIGHEST).T.reshape(lf_s.shape).astype(BF16)
    scatter(nb, bpeer, bdev, bfar, lf_s, lf_r, 12)
    arrived(nb, pj_r, 11)
    pj[b] = added(nb, pj_s[b], pj_r).astype(BF16)
    spread(nb, bdev, bfar, pj, b, 13)
    arrived(nb, lf_r, 12)
    left_here = added(nb, lf_s[b], lf_r).astype(BF16)
    lf_c[...] = left_here

    @pl.when(b == z)
    def _():
        lf[c * nz + z] = left_here

    @pl.when(b != z)
    def _():
        put(lf_c, lf.at[c * nz + b], sends.at[14], recvs.at[14], twin)

    arrived(nb, pj, 13)
    proj = pj[...].astype(F32).reshape(QR, cols_in).astype(BF16)

    slots = nz // 2
    tall_rows = slots * rt_s.shape[1]
    for h in range(4):
        slot = (1 - c if h < 2 else c) * nz + (h % 2) * slots
        at = pl.multiple_of(slot * rt_s.shape[1], tall_rows)
        r = nt(ein[pl.ds(at, tall_rows), :], proj)
        rt_s[pl.ds(slot, slots)] = r.reshape(slots, rt_s.shape[1], QR).astype(BF16)
        if h == 1:
            to_mate(rt_s.at[pl.ds((1 - c) * nz, nz)], rt_p, 15)
    wait_bytes(rt_p, recvs.at[15])
    rt_z[...] = (rt_s[pl.ds(c * nz, nz)].astype(F32) + rt_p[...].astype(F32)).astype(BF16)
    leaves(rt_z, rt_l, l_send, l_recv)

    @pl.when(b != z)
    def _():
        wait_bytes(lf_c, recvs.at[14])
        wait_bytes(lf_c, sends.at[14])

    spread(nz, zdev, zfar, lf, c * nz + z, 17)
    own = gather_in(rt_z, rt_l, rt_a, rt_r, l_recv, j_send, j_recv)
    rt[c * nz + z] = roots(own, rt_r, j_recv)
    slot_rt = slot_of(rt)
    launch(slot_rt, 18, g_recv)
    arrived(nz, lf, 17)
    to_mate(lf.at[pl.ds(c * nz, nz)], lf.at[pl.ds(c * nz, nz)], 19)
    relay(slot_rt, rt, 18, g_recv)
    landed(rt, 18)
    to_mate(rt.at[pl.ds(c * nz, nz)], rt.at[pl.ds(c * nz, nz)], 20)

    loads[6].wait()
    loads[7].wait()
    loads[8].wait()
    wait_bytes(lf.at[pl.ds(0, nz)], recvs.at[19])
    left = lf[...].astype(F32).reshape(gr.shape[1], QR).astype(BF16)
    tk_s[:, :, QR:] = nn(gr[...], left).reshape(nb, -1, QR)
    half = act.shape[1] // 2
    tokens = act.shape[0]
    wait_bytes(rt.at[pl.ds(0, nz)], recvs.at[20])
    tok = None
    for i in range(2):
        right = rt[pl.ds(i * nz, nz)].astype(F32).reshape(half, QR).astype(BF16)
        t = nn(act[:, i * half : (i + 1) * half], right)
        tok = t if tok is None else tok + t
    tk_s[:, :, :QR] = tok.reshape(nb, -1, QR)
    scatter(nb, bpeer, bdev, bfar, tk_s, tk_r, 21)

    here = d * tokens + iota((tokens, lens.shape[1]), 0)
    length = lens[...].astype(F32)
    earlier = jnp.where(
        iota((lens.shape[1],) * 2, 0) < iota((lens.shape[1],) * 2, 1), 1.0, 0.0
    ).astype(BF16)
    start = nn(jnp.broadcast_to(length, (8, lens.shape[1])).astype(BF16), earlier)[0:1, :]
    stop = start + length
    place = here.astype(F32)
    member = jnp.where((place >= start) & (place < stop), 1.0, 0.0).astype(F32)
    pick = jnp.where(
        lax.div(iota((QR, 128), 0), RANK) == iota((QR, 128), 1), 1.0, 0.0
    ).astype(F32)

    arrived(nb, tk_r, 21)
    both = added(nb, tk_s[b], tk_r)
    sc[b] = nn(both[:, :QR] * both[:, QR:], pick, HIGHEST)
    spread(nb, bdev, bfar, sc, b, 22)
    arrived(nb, sc, 22)
    every = sc[...].reshape(tokens, 128)
    scores_o[...] = every.T[:QUERIES, :]
    dc_s[...] = tn(every, member, HIGHEST)[0:QUERIES, :]
    to_mate(dc_s, dc_p, 23)
    wait_bytes(dc_p, recvs.at[23])
    dc_z[...] = dc_s[...] + dc_p[...]
    for k in zfar:
        put(dc_z, dc_r.at[k], sends.at[24], recvs.at[24], zdev(k))
    sent.append((dc_r.at[pl.ds(0, nz - 1)], sends.at[24]))
    arrived(nz, dc_r, 24)
    docs = added(nz, dc_z[...], dc_r)
    doc_o[...] = docs
    for ref, sem in sent:
        wait_bytes(ref, sem)


def local(nb, nz, eig_in, eig_out, eigvals, out_factors, in_factors, test_matrix, activations, gradients, doc_lengths):
    ra, cj = eig_in.shape
    ri, ca = eig_out.shape
    tokens = activations.shape[0]
    docs = doc_lengths.shape[0]
    nd = 2 * nz
    vm = pltpu.VMEM
    scratch = [
        vm((ra, cj), BF16),
        vm((ri, ca), BF16),
        vm((ri, cj), BF16),
        vm(out_factors.shape, BF16),
        vm((RANK, cj), BF16),
        vm(activations.shape, BF16),
        vm(gradients.shape, BF16),
        vm((1, docs), jnp.int32),
        vm((nd, ra // nd, QC), BF16),
        vm((QC, cj), F32),
        vm((ri, cj), F32),
        vm((QUERIES, cj, QR), BF16),
        vm((QUERIES, ri, cj), BF16),
        vm((nb, QC // nb, cj), BF16),
        vm((nb, QC // nb, cj), BF16),
        vm((nb, QC // nb, cj), BF16),
        vm((nd, ri // nd, QC), BF16),
        vm((nz, ri // nd, QC), BF16),
        vm((nz, ri // nd, QC), BF16),
        vm((15, ri // nd, QC), BF16),
        vm((4, ri // nd, QC), BF16),
        vm((4, ri // nd, QC), BF16),
        vm((nd, ri // nd, QC), BF16),
        vm((nd, ri // nd, QR), BF16),
        vm((nz, ri // nd, QR), BF16),
        vm((nz, ri // nd, QR), BF16),
        vm((nz, ri // nd, QR), BF16),
        vm((nd, ri // nd, QR), BF16),
        vm((RANK, QR), F32),
        vm((nb, RANK, QR), F32),
        vm((nb, QR // nb, cj), BF16),
        vm((nb, QR // nb, cj), BF16),
        vm((nb, QR // nb, cj), BF16),
        vm((nb, ca // nb, QR), BF16),
        vm((nb, ca // nb, QR), BF16),
        vm((ca // nb, QR), BF16),
        vm((nd, ca // nb, QR), BF16),
        vm((nd, ra // nd, QR), BF16),
        vm((nz, ra // nd, QR), BF16),
        vm((nz, ra // nd, QR), BF16),
        vm((15, ra // nd, QR), BF16),
        vm((4, ra // nd, QR), BF16),
        vm((4, ra // nd, QR), BF16),
        vm((nd, ra // nd, QR), BF16),
        vm((nb, tokens // nb, 2 * QR), F32),
        vm((nb, tokens // nb, 2 * QR), F32),
        vm((nb, tokens // nb, 128), F32),
        vm((QUERIES, docs), F32),
        vm((QUERIES, docs), F32),
        vm((QUERIES, docs), F32),
        vm((nz, QUERIES, docs), F32),
        pltpu.SemaphoreType.DMA((9,)),
        pltpu.SemaphoreType.DMA(()),
        pltpu.SemaphoreType.DMA((nz,)),
        pltpu.SemaphoreType.DMA(()),
        pltpu.SemaphoreType.DMA((nz,)),
        pltpu.SemaphoreType.DMA(()),
        pltpu.SemaphoreType.DMA((5,)),
        pltpu.SemaphoreType.DMA(()),
        pltpu.SemaphoreType.DMA(()),
        pltpu.SemaphoreType.DMA((4,)),
        pltpu.SemaphoreType.DMA(()),
        pltpu.SemaphoreType.DMA((5,)),
        pltpu.SemaphoreType.DMA(()),
        pltpu.SemaphoreType.DMA(()),
        pltpu.SemaphoreType.DMA((4,)),
        pltpu.SemaphoreType.DMA((25,)),
        pltpu.SemaphoreType.DMA((25,)),
    ]
    scores, influence = pl.pallas_call(
        functools.partial(body, nb, nz),
        out_shape=(
            jax.ShapeDtypeStruct((QUERIES, tokens), F32),
            jax.ShapeDtypeStruct((QUERIES, docs), F32),
        ),
        in_specs=[pl.BlockSpec(memory_space=pl.ANY)] * 9,
        out_specs=(pl.BlockSpec(memory_space=pltpu.VMEM), pl.BlockSpec(memory_space=pltpu.VMEM)),
        scratch_shapes=scratch,
        compiler_params=pltpu.CompilerParams(
            collective_id=0, has_side_effects=True, vmem_limit_bytes=60 * 1024 * 1024
        ),
        name="influence",
    )(
        eig_in,
        eig_out,
        eigvals,
        out_factors,
        in_factors,
        test_matrix.T,
        activations,
        gradients,
        doc_lengths.reshape(1, docs),
    )
    def leave(a, b, x, y):
        x[...] = a[...]
        y[...] = b[...]

    scores, influence = pl.pallas_call(
        leave,
        out_shape=(
            jax.ShapeDtypeStruct(scores.shape, F32),
            jax.ShapeDtypeStruct(influence.shape, F32),
        ),
        name="leave",
    )(scores, influence)
    return scores.T, influence.T


def solution(mesh):
    nb = mesh.shape["basis"]
    nz = mesh.shape["docs"] // 2
    return jax.shard_map(
        functools.partial(local, nb, nz),
        mesh=mesh,
        in_specs=(
            P("basis", "docs"),
            P("basis", "docs"),
            P("basis", "docs"),
            P("docs", None),
            P(("basis", "docs"), None),
            P("docs", None),
            P("docs", "basis"),
            P("docs", "basis"),
            P(),
        ),
        out_specs=(P("docs", None), P()),
        check_vma=False,
    )
```

```python
import functools

import jax
import jax.numpy as jnp
from jax import lax
from jax.experimental import pallas as pl
from jax.experimental.pallas import tpu as pltpu
from jax.sharding import PartitionSpec as P

QUERIES = 4
LQ = 64
RANK = 32
QR = QUERIES * RANK
QC = QUERIES * LQ
HC = QC // 2
DAMPING = 0.1
MESH = pl.DeviceIdType.MESH
HIGHEST = lax.Precision.HIGHEST
F32 = jnp.float32
BF16 = jnp.bfloat16


def nn(a, b, precision=None):
    return lax.dot_general(a, b, (((1,), (0,)), ((), ())), precision=precision, preferred_element_type=F32)


def nt(a, b, precision=None):
    return lax.dot_general(a, b, (((1,), (1,)), ((), ())), precision=precision, preferred_element_type=F32)


def tn(a, b, precision=None):
    return lax.dot_general(a, b, (((0,), (0,)), ((), ())), precision=precision, preferred_element_type=F32)


def iota(shape, axis):
    return lax.broadcasted_iota(jnp.int32, shape, axis)


def ring(k, n):
    return min(k, n - k)


def far_first(n):
    return sorted(range(1, n), key=lambda k: -ring(k, n))


def far_first_grid(n, side):
    if side == 1:
        return far_first(n)
    return sorted(range(1, n), key=lambda k: -ring(k // side, side) - ring(k % side, side))


def tree(n):
    if n == 16:
        return (6, -6, 3, -3), ((6, 2),)
    if n == 4:
        return (), ((0, 2),)
    return (), ()


def wait_bytes(ref, sem):
    pltpu.make_async_copy(ref, ref, sem).wait()


def body(
    nb,
    nz,
    ein_h,
    eout_h,
    lam_h,
    of_h,
    inf_h,
    te_h,
    act_h,
    gr_h,
    len_h,
    scores_o,
    doc_o,
    ein,
    eout,
    lam,
    outf,
    te,
    act,
    gr,
    lens,
    xin,
    acc,
    wgt,
    tsel,
    mom,
    pin_s,
    pin_r,
    rin,
    po_s,
    po_p,
    po_z,
    po_l,
    po_a,
    po_r,
    ro,
    sk_s,
    sk_p,
    sk_z,
    sk_r,
    sk,
    gm_s,
    gm_r,
    pj_s,
    pj_r,
    pj,
    lf_s,
    lf_r,
    lf_c,
    lf,
    rt_s,
    rt_p,
    rt_z,
    rt_l,
    rt_a,
    rt_r,
    rt,
    tk_s,
    tk_r,
    sc,
    dc_s,
    dc_p,
    dc_z,
    dc_r,
    in_sem,
    a_send,
    a_recv,
    f_send,
    f_recv,
    l_send,
    l_recv,
    j_send,
    j_recv,
    g_recv,
    p_send,
    p_recv,
    q_send,
    q_recv,
    h_recv,
    sends,
    recvs,
):
    b = lax.axis_index("basis")
    d = lax.axis_index("docs")
    z = lax.div(d, 2)
    c = lax.rem(d, 2)
    mate = {"docs": z * 2 + (1 - c)}
    sent = []

    def zdev(k):
        return {"docs": lax.rem(z + k + nz, nz) * 2 + c}

    side = 4 if nb == 16 else 2 if nb == 4 else 1

    def bpeer(k):
        if side == 1:
            return lax.rem(b + k, nb)
        across = lax.rem(lax.div(b, side) + k // side, side)
        return across * side + lax.rem(lax.rem(b, side) + k % side, side)

    def zpeer(k):
        return lax.rem(z + k, nz)

    def bdev(k):
        return {"basis": bpeer(k)}

    zfar, bfar = far_first(nz), far_first_grid(nb, side)

    def put(src, dst, s, r, dev):
        pltpu.make_async_remote_copy(
            src_ref=src, dst_ref=dst, send_sem=s, recv_sem=r, device_id=dev, device_id_type=MESH
        ).start()

    def to_mate(src, dst, ch):
        put(src, dst, sends.at[ch], recvs.at[ch], mate)
        sent.append((src, sends.at[ch]))

    def scatter(n, peer, dev, far, src, dst, ch):
        for k in far:
            put(
                src.at[peer(k)],
                dst.at[k],
                sends.at[ch],
                recvs.at[ch],
                dev(k),
            )
        sent.append((dst.at[pl.ds(0, n - 1)], sends.at[ch]))

    def spread(n, dev, far, ref, where, ch):
        for k in far:
            put(ref.at[where], ref.at[where], sends.at[ch], recvs.at[ch], dev(k))
        sent.append((ref.at[pl.ds(0, n - 1)], sends.at[ch]))

    def arrived(n, ref, ch):
        wait_bytes(ref.at[pl.ds(0, n - 1)], recvs.at[ch])

    def added(n, first, ref):
        total = first.astype(F32)
        for k in range(1, n):
            total = total + ref[k].astype(F32)
        return total

    loads = []
    for i, (src, dst) in enumerate(
        (
            (inf_h.at[:, pl.ds(0, HC)], xin.at[0, d]),
            (eout_h, eout),
            (of_h, outf),
            (ein_h, ein),
            (lam_h, lam),
            (te_h, te),
            (act_h, act),
            (gr_h, gr),
            (len_h, lens),
            (inf_h.at[:, pl.ds(HC, HC)], xin.at[1, d]),
        )
    ):
        cp = pltpu.make_async_copy(src, dst, in_sem.at[i])
        cp.start()
        loads.append(cp)

    barrier = pltpu.get_barrier_semaphore()
    for k in zfar:
        pl.semaphore_signal(barrier, inc=1, device_id=zdev(k), device_id_type=MESH)
    for k in bfar:
        pl.semaphore_signal(barrier, inc=1, device_id=bdev(k), device_id_type=MESH)
    pl.semaphore_signal(barrier, inc=1, device_id=mate, device_id_type=MESH)
    twin = {"basis": z, "docs": b * 2 + c}

    @pl.when(b != z)
    def _():
        pl.semaphore_signal(barrier, inc=1, device_id=twin, device_id_type=MESH)


    loads[1].wait()
    loads[2].wait()
    part = nn(eout[...], outf[...])
    po_s[...] = part.reshape(po_s.shape)

    loads[4].wait()
    wgt[...] = 1.0 / (lam[...].astype(F32) + DAMPING)
    loads[5].wait()
    wide = jnp.concatenate([te[...].astype(F32)] * QUERIES, axis=0).T
    for q in range(QUERIES):
        tsel[q] = jnp.where(lax.div(iota(wide.shape, 1), RANK) == q, wide, 0.0).astype(BF16)

    pl.semaphore_wait(barrier, nz + nb - 1 + jnp.where(b != z, 1, 0))

    jumps, extra = tree(nz)
    near = (1, -1) if nz > 2 else (1,)
    beyond = dict(extra)

    def forward(slot, off, s, r):
        for step in near + ((beyond[off],) if off in beyond else ()):
            put(slot(off), slot(off), s, r(off + step), zdev(step))

    def tree_gather(slot, s, r):
        for j in jumps:
            put(slot(0), slot(0), s, r(j), zdev(j))
        forward(slot, 0, s, r)

    def slot_in(h):
        return lambda off: xin.at[h, lax.rem(z - off + nz, nz) * 2 + c]

    def slot_of(ref):
        return lambda off: ref.at[c * nz + lax.rem(z - off + nz, nz)]

    centers = jumps + (0,)

    def leaves(parts, ref, s, r):
        count = 0
        for i, e in enumerate(centers):
            steps = near + ((beyond[e],) if e in beyond else ())
            for m, step in enumerate(steps):
                target = lax.rem(z - e - step + 2 * nz, nz)
                put(parts.at[target], ref.at[3 * i + m], s, r.at[i], zdev(-step))
                count += 1
        sent.append((parts.at[pl.ds(0, count)], s))

    def gather_in(parts, ref, agg, got, r, js, jr):
        total = None
        for i, e in enumerate(centers):
            steps = near + ((beyond[e],) if e in beyond else ())
            wait_bytes(ref.at[pl.ds(3 * i, len(steps))], r.at[i])
            total = parts[lax.rem(z - e + nz, nz)].astype(F32)
            for m in range(len(steps)):
                total = total + ref[3 * i + m].astype(F32)
            if e != 0:
                agg[i] = total.astype(BF16)
                put(agg.at[i], got.at[i], js, jr, zdev(-e))
        if len(jumps) > 0:
            sent.append((agg.at[pl.ds(0, len(jumps))], js))
        return total

    def roots(total, got, jr):
        if len(jumps) > 0:
            wait_bytes(got.at[pl.ds(0, len(jumps))], jr)
            for i in range(len(jumps)):
                total = total + got[i].astype(F32)
        return total.astype(BF16)

    def relay(slot, ref, ch, rj):
        for j in sorted(jumps, key=abs):
            wait_bytes(slot(j), rj.at[jumps.index(j)])
            forward(slot, j, sends.at[ch], lambda off: recvs.at[ch])
        sent.append((ref.at[pl.ds(0, nz - 1)], sends.at[ch]))

    def launch(slot, ch, rj):
        tree_gather(slot, sends.at[ch], lambda off: rj.at[jumps.index(off)] if off in jumps else recvs.at[ch])

    def landed(ref, ch):
        wait_bytes(ref.at[pl.ds(0, nz - 1 - len(jumps))], recvs.at[ch])

    order = list(near) + ([beyond[0]] if 0 in beyond else [])
    for j in sorted(jumps, key=abs):
        order.append(j)
    for j in sorted(jumps, key=abs):
        order += [j + e for e in near] + ([j + beyond[j]] if j in beyond else [])
    for h in range(2):
        loads[9 * h].wait()
        tree_gather(slot_in(h), a_send.at[h], lambda off: a_recv.at[h, off % nz])
        sent.append((xin.at[h, pl.ds(0, nz - 1)], a_send.at[h]))
        put(xin.at[h, d], xin.at[h, d], f_send.at[h], f_recv.at[h, 0], mate)

    to_mate(po_s.at[pl.ds((1 - c) * nz, nz)], po_p, 0)
    wait_bytes(po_p, recvs.at[0])
    po_z[...] = (po_s[pl.ds(c * nz, nz)] + po_p[...]).astype(BF16)

    leaves(po_z, po_l, p_send, p_recv)

    def take_in(h, offs):
        slot = slot_in(h)
        for off in offs:
            pltpu.make_async_copy(slot(off), slot(off), a_recv.at[h, off % nz]).wait()
            if off in jumps:
                forward(slot, off, a_send.at[h], lambda o: a_recv.at[h, o % nz])
            put(slot(off), slot(off), f_send.at[h], f_recv.at[h, off % nz], mate)

    pieces = xin.shape[1] // 4
    rows = pieces * xin.shape[2]

    def input_rows(h):
        sent.append((xin.at[h, pl.ds(0, nz)], f_send.at[h]))
        for k in range(nz):
            other = lax.rem(z - k + nz, nz) * 2 + 1 - c
            pltpu.make_async_copy(xin.at[h, other], xin.at[h, other], f_recv.at[h, k]).wait()
        for i in range(4):
            x = xin[h, pl.ds(i * pieces, pieces)].astype(F32).reshape(rows, HC).astype(BF16)
            t = tn(x, ein[pl.ds(i * rows, rows), :])
            if i == 0:
                acc[pl.ds(h * HC, HC), :] = t
            elif i < 3:
                acc[pl.ds(h * HC, HC), :] += t
            else:
                t = acc[pl.ds(h * HC, HC), :] + t
                pin_s[h] = t.reshape(pin_s.shape[1:]).astype(BF16)
        scatter(nb, bpeer, bdev, bfar, pin_s.at[h], pin_r.at[h], (2, 1)[h])

    split = len(order) - sum(len(near) + (j in beyond) for j in jumps)
    take_in(0, order[:split])
    out_sum = gather_in(po_z, po_l, po_a, po_r, p_recv, q_send, q_recv)
    take_in(1, order[:split])
    take_in(0, order[split:])
    loads[3].wait()
    input_rows(0)
    take_in(1, order[split:])
    input_rows(1)
    ro[c * nz + z] = roots(out_sum, po_r, q_recv)
    slot_ro = slot_of(ro)
    launch(slot_ro, 3, h_recv)

    for h in range(2):
        arrived(nb, pin_r.at[h], (2, 1)[h])
        rin[h, b] = added(nb, pin_s[h, b], pin_r.at[h]).astype(BF16)
        spread(nb, bdev, bfar, rin.at[h], b, (4, 25)[h])

    relay(slot_ro, ro, 3, h_recv)
    landed(ro, 3)
    to_mate(ro.at[pl.ds(c * nz, nz)], ro.at[pl.ds(c * nz, nz)], 5)
    wait_bytes(ro.at[pl.ds(0, nz)], recvs.at[5])

    rows_out = eout.shape[0]
    cols_in = ein.shape[1]
    step = 128
    per = sk_s.shape[1]
    per_block = step // per
    blocks = nz // per_block
    for h in range(2):
        arrived(nb, rin.at[h], (4, 25)[h])
        rotin = rin[h].astype(F32).reshape(HC, cols_in).astype(BF16)
        for g in range(2):
            who = 1 - c if g == 0 else c
            for i in range(blocks):
                slot = who * nz + i * per_block
                at = pl.multiple_of(slot * per, step)
                block = ro[pl.ds(slot, per_block)].reshape(step, QC).astype(F32)
                block = block[:, h * HC : (h + 1) * HC]
                lane = lax.div(iota(block.shape, 1), LQ)
                total = None
                for q in range(QUERIES // 2):
                    only = jnp.where(lane == q, block, 0.0).astype(BF16)
                    m = (nn(only, rotin) * wgt[pl.ds(at, step), :]).astype(BF16)
                    mom[2 * h + q, pl.ds(at, step), :] = m
                    t = nn(m, tsel[2 * h + q])
                    total = t if total is None else total + t
                total = total.reshape(per_block, per, QR)
                if h == 0:
                    sk_s[pl.ds(slot, per_block)] = total
                else:
                    sk_s[pl.ds(slot, per_block)] += total
            if h == 1 and g == 0:
                to_mate(sk_s.at[pl.ds((1 - c) * nz, nz)], sk_p, 6)
    wait_bytes(sk_p, recvs.at[6])
    sk_z[...] = (sk_s[pl.ds(c * nz, nz)] + sk_p[...]).astype(BF16)
    scatter(nz, zpeer, zdev, zfar, sk_z, sk_r, 7)
    arrived(nz, sk_r, 7)
    sk[c * nz + z] = added(nz, sk_z[z], sk_r).astype(BF16)
    spread(nz, zdev, zfar, sk, c * nz + z, 8)
    arrived(nz, sk, 8)
    to_mate(sk.at[pl.ds(c * nz, nz)], sk.at[pl.ds(c * nz, nz)], 9)
    wait_bytes(sk.at[pl.ds(0, nz)], recvs.at[9])

    sketch = sk[...].reshape(rows_out, QR).astype(F32).T.astype(BF16)
    gram = nt(sketch, sketch)
    lane_q = lax.div(iota((RANK, QR), 1), RANK)
    mine = jnp.zeros((RANK, QR), F32)
    for q in range(QUERIES):
        mine = mine + jnp.where(lane_q == q, gram[q * RANK : (q + 1) * RANK, :], 0.0)
    gm_s[...] = mine
    for k in bfar:
        put(gm_s, gm_r.at[k], sends.at[10], recvs.at[10], bdev(k))
    sent.append((gm_r.at[pl.ds(0, nb - 1)], sends.at[10]))

    raw = jnp.concatenate(
        [nn(sketch[q * RANK : (q + 1) * RANK, :], mom[q]) for q in range(QUERIES)], axis=0
    )
    acc[pl.ds(0, QR), :] = raw
    left_raw = nn(sketch, eout[...])

    arrived(nb, gm_r, 10)
    a0 = added(nb, mine, gm_r)
    group = 8
    spot = iota((group, QR), 0)
    lane_t = lax.div(iota((group, QR), 1), RANK)
    in_q = iota((group, QR), 1) - lane_t * RANK

    def over_lanes(x):
        out = None
        for q in range(QUERIES):
            s = jnp.sum(jnp.where(lane_t == q, x, 0.0), axis=1, keepdims=True)
            out = jnp.broadcast_to(s, x.shape) if out is None else jnp.where(lane_t == q, s, out)
        return out

    tiles = RANK // group
    a = [a0[t * group : (t + 1) * group, :] for t in range(tiles)]
    e = [jnp.where(in_q == spot + t * group, 1.0, 0.0).astype(F32) for t in range(tiles)]
    for k in range(RANK):
        first, at = k // group, k % group
        col = [over_lanes(jnp.where(in_q == k, a[t], 0.0)) for t in range(first, tiles)]
        pivot = 1.0 / col[0][at : at + 1, :]
        row_a = a[first][at : at + 1, :] * pivot
        row_e = e[first][at : at + 1, :] * pivot
        for t in range(first, tiles):
            f = col[t - first]
            if t == first:
                f = jnp.where(spot > at, f, 0.0)
            a[t] = a[t] - f * row_a
            e[t] = e[t] - f * row_e
    inv = jnp.concatenate(
        [
            e[t] / jnp.sqrt(over_lanes(jnp.where(in_q == spot + t * group, a[t], 0.0)))
            for t in range(tiles)
        ],
        axis=0,
    )
    tall = jnp.concatenate([inv] * QUERIES, axis=0)
    same = lax.div(iota((QR, QR), 0), RANK) == lax.div(iota((QR, QR), 1), RANK)
    solve = jnp.where(same, tall, 0.0)

    pj_s[...] = nn(solve, acc[pl.ds(0, QR), :], HIGHEST).reshape(pj_s.shape).astype(BF16)
    scatter(nb, bpeer, bdev, bfar, pj_s, pj_r, 11)
    lf_s[...] = nn(solve, left_raw, HIGHEST).T.reshape(lf_s.shape).astype(BF16)
    scatter(nb, bpeer, bdev, bfar, lf_s, lf_r, 12)
    arrived(nb, pj_r, 11)
    pj[b] = added(nb, pj_s[b], pj_r).astype(BF16)
    spread(nb, bdev, bfar, pj, b, 13)
    arrived(nb, lf_r, 12)
    left_here = added(nb, lf_s[b], lf_r).astype(BF16)
    lf_c[...] = left_here

    @pl.when(b == z)
    def _():
        lf[c * nz + z] = left_here

    @pl.when(b != z)
    def _():
        put(lf_c, lf.at[c * nz + b], sends.at[14], recvs.at[14], twin)

    arrived(nb, pj, 13)
    proj = pj[...].astype(F32).reshape(QR, cols_in).astype(BF16)

    slots = nz // 2
    tall_rows = slots * rt_s.shape[1]
    for h in range(4):
        slot = (1 - c if h < 2 else c) * nz + (h % 2) * slots
        at = pl.multiple_of(slot * rt_s.shape[1], tall_rows)
        r = nt(ein[pl.ds(at, tall_rows), :], proj)
        rt_s[pl.ds(slot, slots)] = r.reshape(slots, rt_s.shape[1], QR)
        if h == 1:
            to_mate(rt_s.at[pl.ds((1 - c) * nz, nz)], rt_p, 15)
    wait_bytes(rt_p, recvs.at[15])
    rt_z[...] = (rt_s[pl.ds(c * nz, nz)] + rt_p[...]).astype(BF16)
    leaves(rt_z, rt_l, l_send, l_recv)

    @pl.when(b != z)
    def _():
        wait_bytes(lf_c, recvs.at[14])
        wait_bytes(lf_c, sends.at[14])

    spread(nz, zdev, zfar, lf, c * nz + z, 17)
    own = gather_in(rt_z, rt_l, rt_a, rt_r, l_recv, j_send, j_recv)
    rt[c * nz + z] = roots(own, rt_r, j_recv)
    slot_rt = slot_of(rt)
    launch(slot_rt, 18, g_recv)
    arrived(nz, lf, 17)
    to_mate(lf.at[pl.ds(c * nz, nz)], lf.at[pl.ds(c * nz, nz)], 19)
    relay(slot_rt, rt, 18, g_recv)
    landed(rt, 18)
    to_mate(rt.at[pl.ds(c * nz, nz)], rt.at[pl.ds(c * nz, nz)], 20)

    loads[6].wait()
    loads[7].wait()
    loads[8].wait()
    wait_bytes(lf.at[pl.ds(0, nz)], recvs.at[19])
    left = lf[...].astype(F32).reshape(gr.shape[1], QR).astype(BF16)
    tk_s[:, :, QR:] = nn(gr[...], left).reshape(nb, -1, QR)
    half = act.shape[1] // 2
    tokens = act.shape[0]
    wait_bytes(rt.at[pl.ds(0, nz)], recvs.at[20])
    tok = None
    for i in range(2):
        right = rt[pl.ds(i * nz, nz)].astype(F32).reshape(half, QR).astype(BF16)
        t = nn(act[:, i * half : (i + 1) * half], right)
        tok = t if tok is None else tok + t
    tk_s[:, :, :QR] = tok.reshape(nb, -1, QR)
    scatter(nb, bpeer, bdev, bfar, tk_s, tk_r, 21)

    here = d * tokens + iota((tokens, lens.shape[1]), 0)
    length = lens[...].astype(F32)
    earlier = jnp.where(
        iota((lens.shape[1],) * 2, 0) < iota((lens.shape[1],) * 2, 1), 1.0, 0.0
    ).astype(BF16)
    start = nn(jnp.broadcast_to(length, (8, lens.shape[1])).astype(BF16), earlier)[0:1, :]
    stop = start + length
    place = here.astype(F32)
    member = jnp.where((place >= start) & (place < stop), 1.0, 0.0).astype(F32)
    pick = jnp.where(
        lax.div(iota((QR, 128), 0), RANK) == iota((QR, 128), 1), 1.0, 0.0
    ).astype(F32)

    arrived(nb, tk_r, 21)
    both = added(nb, tk_s[b], tk_r)
    sc[b] = nn(both[:, :QR] * both[:, QR:], pick, HIGHEST)
    spread(nb, bdev, bfar, sc, b, 22)
    arrived(nb, sc, 22)
    every = sc[...].reshape(tokens, 128)
    scores_o[...] = every.T[:QUERIES, :]
    dc_s[...] = tn(every, member, HIGHEST)[0:QUERIES, :]
    to_mate(dc_s, dc_p, 23)
    wait_bytes(dc_p, recvs.at[23])
    dc_z[...] = dc_s[...] + dc_p[...]
    for k in zfar:
        put(dc_z, dc_r.at[k], sends.at[24], recvs.at[24], zdev(k))
    sent.append((dc_r.at[pl.ds(0, nz - 1)], sends.at[24]))
    arrived(nz, dc_r, 24)
    docs = added(nz, dc_z[...], dc_r)
    doc_o[...] = docs
    for ref, sem in sent:
        wait_bytes(ref, sem)


def local(nb, nz, eig_in, eig_out, eigvals, out_factors, in_factors, test_matrix, activations, gradients, doc_lengths):
    ra, cj = eig_in.shape
    ri, ca = eig_out.shape
    tokens = activations.shape[0]
    docs = doc_lengths.shape[0]
    nd = 2 * nz
    vm = pltpu.VMEM
    scratch = [
        vm((ra, cj), BF16),
        vm((ri, ca), BF16),
        vm((ri, cj), BF16),
        vm(out_factors.shape, BF16),
        vm((RANK, cj), BF16),
        vm(activations.shape, BF16),
        vm(gradients.shape, BF16),
        vm((1, docs), jnp.int32),
        vm((2, nd, ra // nd, HC), BF16),
        vm((QC, cj), F32),
        vm((ri, cj), F32),
        vm((QUERIES, cj, QR), BF16),
        vm((QUERIES, ri, cj), BF16),
        vm((2, nb, HC // nb, cj), BF16),
        vm((2, nb, HC // nb, cj), BF16),
        vm((2, nb, HC // nb, cj), BF16),
        vm((nd, ri // nd, QC), F32),
        vm((nz, ri // nd, QC), F32),
        vm((nz, ri // nd, QC), BF16),
        vm((15, ri // nd, QC), BF16),
        vm((4, ri // nd, QC), BF16),
        vm((4, ri // nd, QC), BF16),
        vm((nd, ri // nd, QC), BF16),
        vm((nd, ri // nd, QR), F32),
        vm((nz, ri // nd, QR), F32),
        vm((nz, ri // nd, QR), BF16),
        vm((nz, ri // nd, QR), BF16),
        vm((nd, ri // nd, QR), BF16),
        vm((RANK, QR), F32),
        vm((nb, RANK, QR), F32),
        vm((nb, QR // nb, cj), BF16),
        vm((nb, QR // nb, cj), BF16),
        vm((nb, QR // nb, cj), BF16),
        vm((nb, ca // nb, QR), BF16),
        vm((nb, ca // nb, QR), BF16),
        vm((ca // nb, QR), BF16),
        vm((nd, ca // nb, QR), BF16),
        vm((nd, ra // nd, QR), F32),
        vm((nz, ra // nd, QR), F32),
        vm((nz, ra // nd, QR), BF16),
        vm((15, ra // nd, QR), BF16),
        vm((4, ra // nd, QR), BF16),
        vm((4, ra // nd, QR), BF16),
        vm((nd, ra // nd, QR), BF16),
        vm((nb, tokens // nb, 2 * QR), F32),
        vm((nb, tokens // nb, 2 * QR), F32),
        vm((nb, tokens // nb, 128), F32),
        vm((QUERIES, docs), F32),
        vm((QUERIES, docs), F32),
        vm((QUERIES, docs), F32),
        vm((nz, QUERIES, docs), F32),
        pltpu.SemaphoreType.DMA((10,)),
        pltpu.SemaphoreType.DMA((2,)),
        pltpu.SemaphoreType.DMA((2, nz)),
        pltpu.SemaphoreType.DMA((2,)),
        pltpu.SemaphoreType.DMA((2, nz)),
        pltpu.SemaphoreType.DMA(()),
        pltpu.SemaphoreType.DMA((5,)),
        pltpu.SemaphoreType.DMA(()),
        pltpu.SemaphoreType.DMA(()),
        pltpu.SemaphoreType.DMA((4,)),
        pltpu.SemaphoreType.DMA(()),
        pltpu.SemaphoreType.DMA((5,)),
        pltpu.SemaphoreType.DMA(()),
        pltpu.SemaphoreType.DMA(()),
        pltpu.SemaphoreType.DMA((4,)),
        pltpu.SemaphoreType.DMA((26,)),
        pltpu.SemaphoreType.DMA((26,)),
    ]
    scores, influence = pl.pallas_call(
        functools.partial(body, nb, nz),
        out_shape=(
            jax.ShapeDtypeStruct((QUERIES, tokens), F32),
            jax.ShapeDtypeStruct((QUERIES, docs), F32),
        ),
        in_specs=[pl.BlockSpec(memory_space=pl.ANY)] * 9,
        out_specs=(pl.BlockSpec(memory_space=pltpu.VMEM), pl.BlockSpec(memory_space=pltpu.VMEM)),
        scratch_shapes=scratch,
        compiler_params=pltpu.CompilerParams(
            collective_id=0, has_side_effects=True, vmem_limit_bytes=60 * 1024 * 1024
        ),
        name="influence",
    )(
        eig_in,
        eig_out,
        eigvals,
        out_factors,
        in_factors,
        test_matrix.T,
        activations,
        gradients,
        doc_lengths.reshape(1, docs),
    )
    def leave(a, b, x, y):
        x[...] = a[...]
        y[...] = b[...]

    scores, influence = pl.pallas_call(
        leave,
        out_shape=(
            jax.ShapeDtypeStruct(scores.shape, F32),
            jax.ShapeDtypeStruct(influence.shape, F32),
        ),
        name="leave",
    )(scores, influence)
    return scores.T, influence.T


def solution(mesh):
    nb = mesh.shape["basis"]
    nz = mesh.shape["docs"] // 2
    return jax.shard_map(
        functools.partial(local, nb, nz),
        mesh=mesh,
        in_specs=(
            P("basis", "docs"),
            P("basis", "docs"),
            P("basis", "docs"),
            P("docs", None),
            P(("basis", "docs"), None),
            P("docs", None),
            P("docs", "basis"),
            P("docs", "basis"),
            P(),
        ),
        out_specs=(P("docs", None), P()),
        check_vma=False,
    )
```

```python
import functools

import jax
import jax.numpy as jnp
from jax import lax
from jax.experimental import pallas as pl
from jax.experimental.pallas import tpu as pltpu
from jax.sharding import PartitionSpec as P

QUERIES = 4
LQ = 64
RANK = 32
QR = QUERIES * RANK
QC = QUERIES * LQ
HC = QC // 2
DAMPING = 0.1
MESH = pl.DeviceIdType.MESH
HIGHEST = lax.Precision.HIGHEST
F32 = jnp.float32
BF16 = jnp.bfloat16


def nn(a, b, precision=None):
    return lax.dot_general(a, b, (((1,), (0,)), ((), ())), precision=precision, preferred_element_type=F32)


def nt(a, b, precision=None):
    return lax.dot_general(a, b, (((1,), (1,)), ((), ())), precision=precision, preferred_element_type=F32)


def tn(a, b, precision=None):
    return lax.dot_general(a, b, (((0,), (0,)), ((), ())), precision=precision, preferred_element_type=F32)


def iota(shape, axis):
    return lax.broadcasted_iota(jnp.int32, shape, axis)


def ring(k, n):
    return min(k, n - k)


def far_first(n):
    return sorted(range(1, n), key=lambda k: -ring(k, n))


def far_first_grid(n, side):
    if side == 1:
        return far_first(n)
    return sorted(range(1, n), key=lambda k: -ring(k // side, side) - ring(k % side, side))


def tree(n):
    if n == 16:
        return (6, -6, 3, -3), ((6, 2),)
    if n == 4:
        return (), ((0, 2),)
    return (), ()


def wait_bytes(ref, sem):
    pltpu.make_async_copy(ref, ref, sem).wait()


def body(
    nb,
    nz,
    ein_h,
    eout_h,
    lam_h,
    of_h,
    inf_h,
    te_h,
    act_h,
    gr_h,
    len_h,
    scores_o,
    doc_o,
    ein,
    eout,
    lam,
    outf,
    te,
    act,
    gr,
    lens,
    xin,
    acc,
    wgt,
    tsel,
    mom,
    pin_s,
    pin_r,
    rin,
    po_s,
    po_p,
    po_z,
    po_l,
    po_a,
    po_r,
    ro,
    sk_s,
    sk_p,
    sk_z,
    sk_r,
    sk,
    gm_s,
    gm_r,
    pj_s0,
    pj_s1,
    pj_r0,
    pj_r1,
    pj0,
    pj1,
    lf_s,
    lf_r,
    lf_c,
    lf,
    rt_s,
    rt_p,
    rt_z,
    rt_l,
    rt_a,
    rt_r,
    rt,
    tk_s,
    tk_r,
    sc,
    dc_s,
    dc_p,
    dc_z,
    dc_r,
    in_sem,
    a_send,
    a_recv,
    f_send,
    f_recv,
    l_send,
    l_recv,
    j_send,
    j_recv,
    g_recv,
    p_send,
    p_recv,
    q_send,
    q_recv,
    h_recv,
    k_recv,
    sends,
    recvs,
):
    b = lax.axis_index("basis")
    d = lax.axis_index("docs")
    z = lax.div(d, 2)
    c = lax.rem(d, 2)
    mate = {"docs": z * 2 + (1 - c)}
    sent = []

    def zdev(k):
        return {"docs": lax.rem(z + k + nz, nz) * 2 + c}

    side = 4 if nb == 16 else 2 if nb == 4 else 1

    def bpeer(k):
        if side == 1:
            return lax.rem(b + k, nb)
        across = lax.rem(lax.div(b, side) + k // side, side)
        return across * side + lax.rem(lax.rem(b, side) + k % side, side)

    def zpeer(k):
        return lax.rem(z + k, nz)

    def bdev(k):
        return {"basis": bpeer(k)}

    zfar, bfar = far_first(nz), far_first_grid(nb, side)

    def put(src, dst, s, r, dev):
        pltpu.make_async_remote_copy(
            src_ref=src, dst_ref=dst, send_sem=s, recv_sem=r, device_id=dev, device_id_type=MESH
        ).start()

    def to_mate(src, dst, ch):
        put(src, dst, sends.at[ch], recvs.at[ch], mate)
        sent.append((src, sends.at[ch]))

    def scatter(n, peer, dev, far, src, dst, ch):
        for k in far:
            put(
                src.at[peer(k)],
                dst.at[k],
                sends.at[ch],
                recvs.at[ch],
                dev(k),
            )
        sent.append((dst.at[pl.ds(0, n - 1)], sends.at[ch]))

    def spread(n, dev, far, ref, where, ch):
        for k in far:
            put(ref.at[where], ref.at[where], sends.at[ch], recvs.at[ch], dev(k))
        sent.append((ref.at[pl.ds(0, n - 1)], sends.at[ch]))

    def arrived(n, ref, ch):
        wait_bytes(ref.at[pl.ds(0, n - 1)], recvs.at[ch])

    def added(n, first, ref):
        total = first.astype(F32)
        for k in range(1, n):
            total = total + ref[k].astype(F32)
        return total

    loads = []
    for i, (src, dst) in enumerate(
        (
            (inf_h.at[:, pl.ds(0, HC)], xin.at[0, d]),
            (eout_h, eout),
            (of_h, outf),
            (ein_h, ein),
            (lam_h, lam),
            (te_h, te),
            (act_h, act),
            (gr_h, gr),
            (len_h, lens),
            (inf_h.at[:, pl.ds(HC, HC)], xin.at[1, d]),
        )
    ):
        cp = pltpu.make_async_copy(src, dst, in_sem.at[i])
        cp.start()
        loads.append(cp)

    barrier = pltpu.get_barrier_semaphore()
    greet = (6, 10, 3, 13, 2, 14, 1, 15) if nz == 16 else zfar
    for k in greet:
        pl.semaphore_signal(barrier, inc=1, device_id=zdev(k), device_id_type=MESH)
    for k in bfar:
        pl.semaphore_signal(barrier, inc=1, device_id=bdev(k), device_id_type=MESH)
    pl.semaphore_signal(barrier, inc=1, device_id=mate, device_id_type=MESH)
    twin = {"basis": z, "docs": b * 2 + c}

    loads[1].wait()
    loads[2].wait()
    part = nn(eout[...], outf[...])
    po_s[...] = part.reshape(po_s.shape)

    loads[4].wait()
    wgt[...] = 1.0 / (lam[...].astype(F32) + DAMPING)
    loads[5].wait()
    wide = jnp.concatenate([te[...].astype(F32)] * QUERIES, axis=0).T
    for q in range(QUERIES):
        tsel[q] = jnp.where(lax.div(iota(wide.shape, 1), RANK) == q, wide, 0.0).astype(BF16)

    pl.semaphore_wait(barrier, len(greet) + nb)

    jumps, extra = tree(nz)
    near = (1, -1) if nz > 2 else (1,)
    beyond = dict(extra)

    def forward(slot, off, s, r):
        for step in near + ((beyond[off],) if off in beyond else ()):
            put(slot(off), slot(off), s, r(off + step), zdev(step))

    def tree_gather(slot, s, r):
        for j in jumps:
            put(slot(0), slot(0), s, r(j), zdev(j))
        forward(slot, 0, s, r)

    def slot_in(h):
        return lambda off: xin.at[h, lax.rem(z - off + nz, nz) * 2 + c]

    def slot_of(ref):
        return lambda off: ref.at[c * nz + lax.rem(z - off + nz, nz)]

    centers = jumps + (0,)

    def leaves(parts, ref, s, r):
        count = 0
        for i, e in enumerate(centers):
            steps = near + ((beyond[e],) if e in beyond else ())
            for m, step in enumerate(steps):
                target = lax.rem(z - e - step + 2 * nz, nz)
                put(parts.at[target], ref.at[3 * i + m], s, r.at[i], zdev(-step))
                count += 1
        sent.append((parts.at[pl.ds(0, count)], s))

    def gather_in(parts, ref, agg, got, r, js, jr):
        total = None
        for i, e in enumerate(centers):
            steps = near + ((beyond[e],) if e in beyond else ())
            wait_bytes(ref.at[pl.ds(3 * i, len(steps))], r.at[i])
            total = parts[lax.rem(z - e + nz, nz)].astype(F32)
            for m in range(len(steps)):
                total = total + ref[3 * i + m].astype(F32)
            if e != 0:
                agg[i] = total.astype(BF16)
                put(agg.at[i], got.at[i], js, jr, zdev(-e))
        if len(jumps) > 0:
            sent.append((agg.at[pl.ds(0, len(jumps))], js))
        return total

    def roots(total, got, jr):
        if len(jumps) > 0:
            wait_bytes(got.at[pl.ds(0, len(jumps))], jr)
            for i in range(len(jumps)):
                total = total + got[i].astype(F32)
        return total.astype(BF16)

    def relay(slot, ref, ch, rj):
        for j in sorted(jumps, key=abs):
            wait_bytes(slot(j), rj.at[jumps.index(j)])
            forward(slot, j, sends.at[ch], lambda off: recvs.at[ch])
        sent.append((ref.at[pl.ds(0, nz - 1)], sends.at[ch]))

    def launch(slot, ch, rj):
        tree_gather(slot, sends.at[ch], lambda off: rj.at[jumps.index(off)] if off in jumps else recvs.at[ch])

    def landed(ref, ch):
        wait_bytes(ref.at[pl.ds(0, nz - 1 - len(jumps))], recvs.at[ch])

    order = list(near) + ([beyond[0]] if 0 in beyond else [])
    for j in sorted(jumps, key=abs):
        order.append(j)
    for j in sorted(jumps, key=abs):
        order += [j + e for e in near] + ([j + beyond[j]] if j in beyond else [])
    for h in range(2):
        loads[9 * h].wait()
        tree_gather(slot_in(h), a_send.at[h], lambda off: a_recv.at[h, off % nz])
        sent.append((xin.at[h, pl.ds(0, nz - 1)], a_send.at[h]))
        put(xin.at[h, d], xin.at[h, d], f_send.at[h], f_recv.at[h, 0], mate)

    to_mate(po_s.at[pl.ds((1 - c) * nz, nz)], po_p, 0)
    wait_bytes(po_p, recvs.at[0])
    po_z[...] = (po_s[pl.ds(c * nz, nz)] + po_p[...]).astype(BF16)

    leaves(po_z, po_l, p_send, p_recv)

    def take_in(h, offs):
        slot = slot_in(h)
        for off in offs:
            pltpu.make_async_copy(slot(off), slot(off), a_recv.at[h, off % nz]).wait()
            if off in jumps:
                forward(slot, off, a_send.at[h], lambda o: a_recv.at[h, o % nz])
            put(slot(off), slot(off), f_send.at[h], f_recv.at[h, off % nz], mate)

    pieces = xin.shape[1] // 4
    rows = pieces * xin.shape[2]

    def input_rows(h):
        sent.append((xin.at[h, pl.ds(0, nz)], f_send.at[h]))
        for k in range(nz):
            other = lax.rem(z - k + nz, nz) * 2 + 1 - c
            pltpu.make_async_copy(xin.at[h, other], xin.at[h, other], f_recv.at[h, k]).wait()
        for i in range(4):
            x = xin[h, pl.ds(i * pieces, pieces)].astype(F32).reshape(rows, HC).astype(BF16)
            t = tn(x, ein[pl.ds(i * rows, rows), :])
            if i == 0:
                acc[pl.ds(h * HC, HC), :] = t
            elif i < 3:
                acc[pl.ds(h * HC, HC), :] += t
            else:
                t = acc[pl.ds(h * HC, HC), :] + t
                pin_s[h] = t.reshape(pin_s.shape[1:]).astype(BF16)
        scatter(nb, bpeer, bdev, bfar, pin_s.at[h], pin_r.at[h], (2, 1)[h])

    split = len(order) - sum(len(near) + (j in beyond) for j in jumps)
    take_in(0, order[:split])
    out_sum = gather_in(po_z, po_l, po_a, po_r, p_recv, q_send, q_recv)
    take_in(1, order[:split])
    take_in(0, order[split:])
    loads[3].wait()
    input_rows(0)
    take_in(1, order[split:])
    input_rows(1)
    ro[c * nz + z] = roots(out_sum, po_r, q_recv)
    slot_ro = slot_of(ro)
    launch(slot_ro, 3, h_recv)

    for h in range(2):
        arrived(nb, pin_r.at[h], (2, 1)[h])
        rin[h, b] = added(nb, pin_s[h, b], pin_r.at[h]).astype(BF16)
        spread(nb, bdev, bfar, rin.at[h], b, (4, 25)[h])

    relay(slot_ro, ro, 3, h_recv)
    landed(ro, 3)
    to_mate(ro.at[pl.ds(c * nz, nz)], ro.at[pl.ds(c * nz, nz)], 5)
    wait_bytes(ro.at[pl.ds(0, nz)], recvs.at[5])

    rows_out = eout.shape[0]
    cols_in = ein.shape[1]
    step = 128
    per = sk_s.shape[1]
    per_block = step // per
    blocks = nz // per_block
    for h in range(2):
        arrived(nb, rin.at[h], (4, 25)[h])
        rotin = rin[h].astype(F32).reshape(HC, cols_in).astype(BF16)
        for g in range(2):
            who = 1 - c if g == 0 else c
            for i in range(blocks):
                slot = who * nz + i * per_block
                at = pl.multiple_of(slot * per, step)
                block = ro[pl.ds(slot, per_block)].reshape(step, QC).astype(F32)
                block = block[:, h * HC : (h + 1) * HC]
                lane = lax.div(iota(block.shape, 1), LQ)
                total = None
                for q in range(QUERIES // 2):
                    only = jnp.where(lane == q, block, 0.0).astype(BF16)
                    m = (nn(only, rotin) * wgt[pl.ds(at, step), :]).astype(BF16)
                    mom[2 * h + q, pl.ds(at, step), :] = m
                    t = nn(m, tsel[2 * h + q])
                    total = t if total is None else total + t
                total = total.reshape(per_block, per, QR)
                if h == 0:
                    sk_s[pl.ds(slot, per_block)] = total
                else:
                    sk_s[pl.ds(slot, per_block)] += total
            if h == 1 and g == 0:
                to_mate(sk_s.at[pl.ds((1 - c) * nz, nz)], sk_p, 6)
    wait_bytes(sk_p, recvs.at[6])
    sk_z[...] = (sk_s[pl.ds(c * nz, nz)] + sk_p[...]).astype(BF16)
    scatter(nz, zpeer, zdev, zfar, sk_z, sk_r, 7)
    arrived(nz, sk_r, 7)
    sk[c * nz + z] = added(nz, sk_z[z], sk_r).astype(BF16)
    spread(nz, zdev, zfar, sk, c * nz + z, 8)
    arrived(nz, sk, 8)
    to_mate(sk.at[pl.ds(c * nz, nz)], sk.at[pl.ds(c * nz, nz)], 9)
    wait_bytes(sk.at[pl.ds(0, nz)], recvs.at[9])

    sketch = sk[...].reshape(rows_out, QR).astype(F32).T.astype(BF16)
    gram = nt(sketch, sketch)
    lane_q = lax.div(iota((RANK, QR), 1), RANK)
    mine = jnp.zeros((RANK, QR), F32)
    for q in range(QUERIES):
        mine = mine + jnp.where(lane_q == q, gram[q * RANK : (q + 1) * RANK, :], 0.0)
    gm_s[...] = mine
    for k in bfar:
        put(gm_s, gm_r.at[k], sends.at[10], recvs.at[10], bdev(k))
    sent.append((gm_r.at[pl.ds(0, nb - 1)], sends.at[10]))

    raw = jnp.concatenate(
        [nn(sketch[q * RANK : (q + 1) * RANK, :], mom[q]) for q in range(QUERIES)], axis=0
    )
    acc[pl.ds(0, QR), :] = raw
    left_raw = nn(sketch, eout[...])

    arrived(nb, gm_r, 10)
    a0 = added(nb, mine, gm_r)
    group = 8
    spot = iota((group, QR), 0)
    lane_t = lax.div(iota((group, QR), 1), RANK)
    in_q = iota((group, QR), 1) - lane_t * RANK

    def over_lanes(x):
        out = None
        for q in range(QUERIES):
            s = jnp.sum(jnp.where(lane_t == q, x, 0.0), axis=1, keepdims=True)
            out = jnp.broadcast_to(s, x.shape) if out is None else jnp.where(lane_t == q, s, out)
        return out

    tiles = RANK // group
    a = [a0[t * group : (t + 1) * group, :] for t in range(tiles)]
    e = [jnp.where(in_q == spot + t * group, 1.0, 0.0).astype(F32) for t in range(tiles)]
    for k in range(RANK):
        first, at = k // group, k % group
        col = [over_lanes(jnp.where(in_q == k, a[t], 0.0)) for t in range(first, tiles)]
        pivot = 1.0 / col[0][at : at + 1, :]
        row_a = a[first][at : at + 1, :] * pivot
        row_e = e[first][at : at + 1, :] * pivot
        for t in range(first, tiles):
            f = col[t - first]
            if t == first:
                f = jnp.where(spot > at, f, 0.0)
            a[t] = a[t] - f * row_a
            e[t] = e[t] - f * row_e
    inv = jnp.concatenate(
        [
            e[t] / jnp.sqrt(over_lanes(jnp.where(in_q == spot + t * group, a[t], 0.0)))
            for t in range(tiles)
        ],
        axis=0,
    )
    tall = jnp.concatenate([inv] * QUERIES, axis=0)
    same = lax.div(iota((QR, QR), 0), RANK) == lax.div(iota((QR, QR), 1), RANK)
    solve = jnp.where(same, tall, 0.0)

    pjs, pjr, pjo = (pj_s0, pj_s1), (pj_r0, pj_r1), (pj0, pj1)
    wide0 = pj_s0.shape[2]
    parts_of = (pl.ds(0, wide0), pl.ds(wide0, cols_in - wide0))
    for h in range(2):
        ortho = nn(solve, acc[pl.ds(0, QR), parts_of[h]], HIGHEST)
        pjs[h][...] = ortho.reshape(pjs[h].shape).astype(BF16)
        scatter(nb, bpeer, bdev, bfar, pjs[h], pjr[h], (11, 26)[h])
    lf_s[...] = nn(solve, left_raw, HIGHEST).T.reshape(lf_s.shape).astype(BF16)
    scatter(nb, bpeer, bdev, bfar, lf_s, lf_r, 12)
    for h in range(2):
        arrived(nb, pjr[h], (11, 26)[h])
        pjo[h][b] = added(nb, pjs[h][b], pjr[h]).astype(BF16)
        spread(nb, bdev, bfar, pjo[h], b, (13, 27)[h])
    arrived(nb, lf_r, 12)
    left_here = added(nb, lf_s[b], lf_r).astype(BF16)
    lf_c[...] = left_here

    @pl.when(b == z)
    def _():
        lf[c * nz + z] = left_here

    @pl.when(b != z)
    def _():
        put(lf_c, lf.at[c * nz + b], sends.at[14], recvs.at[14], twin)

    slots = nz // 2
    tall_rows = slots * rt_s.shape[1]
    for h in range(2):
        arrived(nb, pjo[h], (13, 27)[h])
        proj = pjo[h][...].astype(F32).reshape(QR, -1).astype(BF16)
        for g in range(4):
            slot = (1 - c if g < 2 else c) * nz + (g % 2) * slots
            at = pl.multiple_of(slot * rt_s.shape[1], tall_rows)
            r = nt(ein[pl.ds(at, tall_rows), parts_of[h]], proj).reshape(slots, rt_s.shape[1], QR)
            if h == 0:
                rt_s[pl.ds(slot, slots)] = r
            else:
                rt_s[pl.ds(slot, slots)] += r
            if h == 1 and g == 1:
                to_mate(rt_s.at[pl.ds((1 - c) * nz, nz)], rt_p, 15)
    wait_bytes(rt_p, recvs.at[15])
    rt_z[...] = (rt_s[pl.ds(c * nz, nz)] + rt_p[...]).astype(BF16)
    leaves(rt_z, rt_l, l_send, l_recv)

    @pl.when(b != z)
    def _():
        wait_bytes(lf_c, recvs.at[14])
        wait_bytes(lf_c, sends.at[14])

    slot_lf = slot_of(lf)
    launch(slot_lf, 17, k_recv)
    own = gather_in(rt_z, rt_l, rt_a, rt_r, l_recv, j_send, j_recv)
    relay(slot_lf, lf, 17, k_recv)
    rt[c * nz + z] = roots(own, rt_r, j_recv)
    slot_rt = slot_of(rt)
    launch(slot_rt, 18, g_recv)
    relay(slot_rt, rt, 18, g_recv)
    landed(lf, 17)
    to_mate(lf.at[pl.ds(c * nz, nz)], lf.at[pl.ds(c * nz, nz)], 19)
    landed(rt, 18)
    to_mate(rt.at[pl.ds(c * nz, nz)], rt.at[pl.ds(c * nz, nz)], 20)

    loads[6].wait()
    loads[7].wait()
    loads[8].wait()
    half = act.shape[1] // 2
    tokens = act.shape[0]

    def token_half(who):
        right = rt[pl.ds(who * nz, nz)].astype(F32).reshape(half, QR).astype(BF16)
        return nn(act[:, pl.ds(pl.multiple_of(who * half, half), half)], right)

    tok = token_half(c)
    wait_bytes(lf.at[pl.ds(0, nz)], recvs.at[19])
    left = lf[...].astype(F32).reshape(gr.shape[1], QR).astype(BF16)
    tk_s[:, :, QR:] = nn(gr[...], left).reshape(nb, -1, QR)
    wait_bytes(rt.at[pl.ds(0, nz)], recvs.at[20])
    tok = tok + token_half(1 - c)
    tk_s[:, :, :QR] = tok.reshape(nb, -1, QR)
    scatter(nb, bpeer, bdev, bfar, tk_s, tk_r, 21)

    here = d * tokens + iota((tokens, lens.shape[1]), 0)
    length = lens[...].astype(F32)
    earlier = jnp.where(
        iota((lens.shape[1],) * 2, 0) < iota((lens.shape[1],) * 2, 1), 1.0, 0.0
    ).astype(BF16)
    start = nn(jnp.broadcast_to(length, (8, lens.shape[1])).astype(BF16), earlier)[0:1, :]
    stop = start + length
    place = here.astype(F32)
    member = jnp.where((place >= start) & (place < stop), 1.0, 0.0).astype(F32)
    pick = jnp.where(
        lax.div(iota((QR, 128), 0), RANK) == iota((QR, 128), 1), 1.0, 0.0
    ).astype(F32)

    arrived(nb, tk_r, 21)
    both = added(nb, tk_s[b], tk_r)
    sc[b] = nn(both[:, :QR] * both[:, QR:], pick, HIGHEST)
    spread(nb, bdev, bfar, sc, b, 22)
    arrived(nb, sc, 22)
    every = sc[...].reshape(tokens, 128)
    scores_o[...] = every.T[:QUERIES, :]
    dc_s[...] = tn(every, member, HIGHEST)[0:QUERIES, :]
    to_mate(dc_s, dc_p, 23)
    wait_bytes(dc_p, recvs.at[23])
    dc_z[...] = dc_s[...] + dc_p[...]
    for k in zfar:
        put(dc_z, dc_r.at[k], sends.at[24], recvs.at[24], zdev(k))
    sent.append((dc_r.at[pl.ds(0, nz - 1)], sends.at[24]))
    arrived(nz, dc_r, 24)
    docs = added(nz, dc_z[...], dc_r)
    doc_o[...] = docs
    for ref, sem in sent:
        wait_bytes(ref, sem)


def local(nb, nz, eig_in, eig_out, eigvals, out_factors, in_factors, test_matrix, activations, gradients, doc_lengths):
    ra, cj = eig_in.shape
    ri, ca = eig_out.shape
    tokens = activations.shape[0]
    docs = doc_lengths.shape[0]
    nd = 2 * nz
    vm = pltpu.VMEM
    wide = (cj // 2 + 127) // 128 * 128
    scratch = [
        vm((ra, cj), BF16),
        vm((ri, ca), BF16),
        vm((ri, cj), BF16),
        vm(out_factors.shape, BF16),
        vm((RANK, cj), BF16),
        vm(activations.shape, BF16),
        vm(gradients.shape, BF16),
        vm((1, docs), jnp.int32),
        vm((2, nd, ra // nd, HC), BF16),
        vm((QC, cj), F32),
        vm((ri, cj), F32),
        vm((QUERIES, cj, QR), BF16),
        vm((QUERIES, ri, cj), BF16),
        vm((2, nb, HC // nb, cj), BF16),
        vm((2, nb, HC // nb, cj), BF16),
        vm((2, nb, HC // nb, cj), BF16),
        vm((nd, ri // nd, QC), F32),
        vm((nz, ri // nd, QC), F32),
        vm((nz, ri // nd, QC), BF16),
        vm((15, ri // nd, QC), BF16),
        vm((4, ri // nd, QC), BF16),
        vm((4, ri // nd, QC), BF16),
        vm((nd, ri // nd, QC), BF16),
        vm((nd, ri // nd, QR), F32),
        vm((nz, ri // nd, QR), F32),
        vm((nz, ri // nd, QR), BF16),
        vm((nz, ri // nd, QR), BF16),
        vm((nd, ri // nd, QR), BF16),
        vm((RANK, QR), F32),
        vm((nb, RANK, QR), F32),
        *(vm((nb, QR // nb, w), BF16) for _ in range(3) for w in (wide, cj - wide)),
        vm((nb, ca // nb, QR), BF16),
        vm((nb, ca // nb, QR), BF16),
        vm((ca // nb, QR), BF16),
        vm((nd, ca // nb, QR), BF16),
        vm((nd, ra // nd, QR), F32),
        vm((nz, ra // nd, QR), F32),
        vm((nz, ra // nd, QR), BF16),
        vm((15, ra // nd, QR), BF16),
        vm((4, ra // nd, QR), BF16),
        vm((4, ra // nd, QR), BF16),
        vm((nd, ra // nd, QR), BF16),
        vm((nb, tokens // nb, 2 * QR), F32),
        vm((nb, tokens // nb, 2 * QR), F32),
        vm((nb, tokens // nb, 128), F32),
        vm((QUERIES, docs), F32),
        vm((QUERIES, docs), F32),
        vm((QUERIES, docs), F32),
        vm((nz, QUERIES, docs), F32),
        pltpu.SemaphoreType.DMA((10,)),
        pltpu.SemaphoreType.DMA((2,)),
        pltpu.SemaphoreType.DMA((2, nz)),
        pltpu.SemaphoreType.DMA((2,)),
        pltpu.SemaphoreType.DMA((2, nz)),
        pltpu.SemaphoreType.DMA(()),
        pltpu.SemaphoreType.DMA((5,)),
        pltpu.SemaphoreType.DMA(()),
        pltpu.SemaphoreType.DMA(()),
        pltpu.SemaphoreType.DMA((4,)),
        pltpu.SemaphoreType.DMA(()),
        pltpu.SemaphoreType.DMA((5,)),
        pltpu.SemaphoreType.DMA(()),
        pltpu.SemaphoreType.DMA(()),
        pltpu.SemaphoreType.DMA((4,)),
        pltpu.SemaphoreType.DMA((4,)),
        pltpu.SemaphoreType.DMA((28,)),
        pltpu.SemaphoreType.DMA((28,)),
    ]
    scores, influence = pl.pallas_call(
        functools.partial(body, nb, nz),
        out_shape=(
            jax.ShapeDtypeStruct((QUERIES, tokens), F32),
            jax.ShapeDtypeStruct((QUERIES, docs), F32),
        ),
        in_specs=[pl.BlockSpec(memory_space=pl.ANY)] * 9,
        out_specs=(pl.BlockSpec(memory_space=pltpu.VMEM), pl.BlockSpec(memory_space=pltpu.VMEM)),
        scratch_shapes=scratch,
        compiler_params=pltpu.CompilerParams(
            collective_id=0, has_side_effects=True, vmem_limit_bytes=60 * 1024 * 1024
        ),
        name="influence",
    )(
        eig_in,
        eig_out,
        eigvals,
        out_factors,
        in_factors,
        test_matrix.T,
        activations,
        gradients,
        doc_lengths.reshape(1, docs),
    )
    def leave(a, b, x, y):
        x[...] = a[...]
        y[...] = b[...]

    scores, influence = pl.pallas_call(
        leave,
        out_shape=(
            jax.ShapeDtypeStruct(scores.shape, F32),
            jax.ShapeDtypeStruct(influence.shape, F32),
        ),
        name="leave",
    )(scores, influence)
    return scores.T, influence.T


def solution(mesh):
    nb = mesh.shape["basis"]
    nz = mesh.shape["docs"] // 2
    return jax.shard_map(
        functools.partial(local, nb, nz),
        mesh=mesh,
        in_specs=(
            P("basis", "docs"),
            P("basis", "docs"),
            P("basis", "docs"),
            P("docs", None),
            P(("basis", "docs"), None),
            P("docs", None),
            P("docs", "basis"),
            P("docs", "basis"),
            P(),
        ),
        out_specs=(P("docs", None), P()),
        check_vma=False,
    )
```

```python
import functools

import jax
import jax.numpy as jnp
from jax import lax
from jax.experimental import pallas as pl
from jax.experimental.pallas import tpu as pltpu
from jax.sharding import PartitionSpec as P

QUERIES = 4
LQ = 64
RANK = 32
QR = QUERIES * RANK
QC = QUERIES * LQ
HC = QC // 2
DAMPING = 0.1
MESH = pl.DeviceIdType.MESH
HIGHEST = lax.Precision.HIGHEST
F32 = jnp.float32
BF16 = jnp.bfloat16


def nn(a, b, precision=None):
    return lax.dot_general(a, b, (((1,), (0,)), ((), ())), precision=precision, preferred_element_type=F32)


def nt(a, b, precision=None):
    return lax.dot_general(a, b, (((1,), (1,)), ((), ())), precision=precision, preferred_element_type=F32)


def tn(a, b, precision=None):
    return lax.dot_general(a, b, (((0,), (0,)), ((), ())), precision=precision, preferred_element_type=F32)


def iota(shape, axis):
    return lax.broadcasted_iota(jnp.int32, shape, axis)


def ring(k, n):
    return min(k, n - k)


def far_first(n):
    return sorted(range(1, n), key=lambda k: -ring(k, n))


def far_first_grid(n, side):
    if side == 1:
        return far_first(n)
    return sorted(range(1, n), key=lambda k: -ring(k // side, side) - ring(k % side, side))


def tree(n):
    if n == 16:
        return (6, -6, 3, -3), ((6, 2),)
    if n == 4:
        return (), ((0, 2),)
    return (), ()


def wait_bytes(ref, sem):
    pltpu.make_async_copy(ref, ref, sem).wait()


def body(
    nb,
    nz,
    ein_h,
    eout_h,
    lam_h,
    of_h,
    inf_h,
    te_h,
    act_h,
    gr_h,
    len_h,
    scores_o,
    doc_o,
    ein,
    eout,
    lam,
    outf,
    te,
    act,
    gr,
    lens,
    xin,
    acc,
    wgt,
    tsel,
    mom,
    pin_s,
    pin_r,
    rin,
    po_s,
    po_p,
    po_z,
    po_l,
    po_a,
    po_r,
    ro,
    sk_s,
    sk_p,
    sk_z,
    sk_r,
    sk,
    gm_s,
    gm_r,
    pj_s0,
    pj_s1,
    pj_r0,
    pj_r1,
    pj0,
    pj1,
    lf_s,
    lf_r,
    lf_c,
    lf,
    rt_s,
    rt_p,
    rt_z,
    rt_l,
    rt_a,
    rt_r,
    rt,
    tk_s,
    tk_r,
    sc,
    dc_s,
    dc_p,
    dc_z,
    dc_r,
    in_sem,
    a_send,
    a_recv,
    f_send,
    f_recv,
    l_send,
    l_recv,
    j_send,
    j_recv,
    g_recv,
    p_send,
    p_recv,
    q_send,
    q_recv,
    h_recv,
    k_recv,
    sends,
    recvs,
):
    b = lax.axis_index("basis")
    d = lax.axis_index("docs")
    z = lax.div(d, 2)
    c = lax.rem(d, 2)
    mate = {"docs": z * 2 + (1 - c)}
    sent = []

    def zdev(k):
        return {"docs": lax.rem(z + k + nz, nz) * 2 + c}

    side = 4 if nb == 16 else 2 if nb == 4 else 1

    def bpeer(k):
        if side == 1:
            return lax.rem(b + k, nb)
        across = lax.rem(lax.div(b, side) + k // side, side)
        return across * side + lax.rem(lax.rem(b, side) + k % side, side)

    def zpeer(k):
        return lax.rem(z + k, nz)

    def bdev(k):
        return {"basis": bpeer(k)}

    zfar, bfar = far_first(nz), far_first_grid(nb, side)

    def put(src, dst, s, r, dev):
        pltpu.make_async_remote_copy(
            src_ref=src, dst_ref=dst, send_sem=s, recv_sem=r, device_id=dev, device_id_type=MESH
        ).start()

    def to_mate(src, dst, ch):
        put(src, dst, sends.at[ch], recvs.at[ch], mate)
        sent.append((src, sends.at[ch]))

    def scatter(n, peer, dev, far, src, dst, ch):
        for k in far:
            put(
                src.at[peer(k)],
                dst.at[k],
                sends.at[ch],
                recvs.at[ch],
                dev(k),
            )
        sent.append((dst.at[pl.ds(0, n - 1)], sends.at[ch]))

    def spread(n, dev, far, ref, where, ch):
        for k in far:
            put(ref.at[where], ref.at[where], sends.at[ch], recvs.at[ch], dev(k))
        sent.append((ref.at[pl.ds(0, n - 1)], sends.at[ch]))

    def arrived(n, ref, ch):
        wait_bytes(ref.at[pl.ds(0, n - 1)], recvs.at[ch])

    def added(n, first, ref):
        total = first.astype(F32)
        for k in range(1, n):
            total = total + ref[k].astype(F32)
        return total

    loads = []
    for i, (src, dst) in enumerate(
        (
            (inf_h.at[:, pl.ds(0, HC)], xin.at[0, d]),
            (eout_h, eout),
            (of_h, outf),
            (ein_h, ein),
            (lam_h, lam),
            (te_h, te),
            (act_h, act),
            (gr_h, gr),
            (len_h, lens),
            (inf_h.at[:, pl.ds(HC, HC)], xin.at[1, d]),
        )
    ):
        cp = pltpu.make_async_copy(src, dst, in_sem.at[i])
        cp.start()
        loads.append(cp)

    barrier = pltpu.get_barrier_semaphore()
    greet = (6, 10, 3, 13, 2, 14, 1, 15) if nz == 16 else zfar
    for k in greet:
        pl.semaphore_signal(barrier, inc=1, device_id=zdev(k), device_id_type=MESH)
    for k in bfar:
        pl.semaphore_signal(barrier, inc=1, device_id=bdev(k), device_id_type=MESH)
    pl.semaphore_signal(barrier, inc=1, device_id=mate, device_id_type=MESH)
    twin = {"basis": z, "docs": b * 2 + c}

    loads[1].wait()
    loads[2].wait()
    part = nn(eout[...], outf[...])
    po_s[...] = part.reshape(po_s.shape)

    loads[4].wait()
    wgt[...] = 1.0 / (lam[...].astype(F32) + DAMPING)
    loads[5].wait()
    wide = jnp.concatenate([te[...].astype(F32)] * QUERIES, axis=0).T
    for q in range(QUERIES):
        tsel[q] = jnp.where(lax.div(iota(wide.shape, 1), RANK) == q, wide, 0.0).astype(BF16)

    pl.semaphore_wait(barrier, len(greet) + nb)

    jumps, extra = tree(nz)
    near = (1, -1) if nz > 2 else (1,)
    beyond = dict(extra)

    def forward(slot, off, s, r):
        for step in near + ((beyond[off],) if off in beyond else ()):
            put(slot(off), slot(off), s, r(off + step), zdev(step))

    def tree_gather(slot, s, r):
        for j in jumps:
            put(slot(0), slot(0), s, r(j), zdev(j))
        forward(slot, 0, s, r)

    def slot_in(h):
        return lambda off: xin.at[h, lax.rem(z - off + nz, nz) * 2 + c]

    def slot_of(ref):
        return lambda off: ref.at[c * nz + lax.rem(z - off + nz, nz)]

    centers = jumps + (0,)

    def leaves(parts, ref, s, r):
        count = 0
        for i, e in enumerate(centers):
            steps = near + ((beyond[e],) if e in beyond else ())
            for m, step in enumerate(steps):
                target = lax.rem(z - e - step + 2 * nz, nz)
                put(parts.at[target], ref.at[3 * i + m], s, r.at[i], zdev(-step))
                count += 1
        sent.append((parts.at[pl.ds(0, count)], s))

    def gather_in(parts, ref, agg, got, r, js, jr):
        total = None
        for i, e in enumerate(centers):
            steps = near + ((beyond[e],) if e in beyond else ())
            wait_bytes(ref.at[pl.ds(3 * i, len(steps))], r.at[i])
            total = parts[lax.rem(z - e + nz, nz)].astype(F32)
            for m in range(len(steps)):
                total = total + ref[3 * i + m].astype(F32)
            if e != 0:
                agg[i] = total.astype(BF16)
                put(agg.at[i], got.at[i], js, jr, zdev(-e))
        if len(jumps) > 0:
            sent.append((agg.at[pl.ds(0, len(jumps))], js))
        return total

    def roots(total, got, jr):
        if len(jumps) > 0:
            wait_bytes(got.at[pl.ds(0, len(jumps))], jr)
            for i in range(len(jumps)):
                total = total + got[i].astype(F32)
        return total.astype(BF16)

    def relay(slot, ref, ch, rj):
        for j in sorted(jumps, key=abs):
            wait_bytes(slot(j), rj.at[jumps.index(j)])
            forward(slot, j, sends.at[ch], lambda off: recvs.at[ch])
        sent.append((ref.at[pl.ds(0, nz - 1)], sends.at[ch]))

    def launch(slot, ch, rj):
        tree_gather(slot, sends.at[ch], lambda off: rj.at[jumps.index(off)] if off in jumps else recvs.at[ch])

    def landed(ref, ch):
        wait_bytes(ref.at[pl.ds(0, nz - 1 - len(jumps))], recvs.at[ch])

    order = list(near) + ([beyond[0]] if 0 in beyond else [])
    for j in sorted(jumps, key=abs):
        order.append(j)
    for j in sorted(jumps, key=abs):
        order += [j + e for e in near] + ([j + beyond[j]] if j in beyond else [])
    for h in range(2):
        loads[9 * h].wait()
        tree_gather(slot_in(h), a_send.at[h], lambda off: a_recv.at[h, off % nz])
        sent.append((xin.at[h, pl.ds(0, nz - 1)], a_send.at[h]))
        put(xin.at[h, d], xin.at[h, d], f_send.at[h], f_recv.at[h, 0], mate)

    to_mate(po_s.at[pl.ds((1 - c) * nz, nz)], po_p, 0)
    wait_bytes(po_p, recvs.at[0])
    po_z[...] = (po_s[pl.ds(c * nz, nz)] + po_p[...]).astype(BF16)

    leaves(po_z, po_l, p_send, p_recv)

    def take_in(h, offs):
        slot = slot_in(h)
        for off in offs:
            pltpu.make_async_copy(slot(off), slot(off), a_recv.at[h, off % nz]).wait()
            if off in jumps:
                forward(slot, off, a_send.at[h], lambda o: a_recv.at[h, o % nz])
            put(slot(off), slot(off), f_send.at[h], f_recv.at[h, off % nz], mate)

    pieces = xin.shape[1] // 4
    rows = pieces * xin.shape[2]

    def input_rows(h):
        sent.append((xin.at[h, pl.ds(0, nz)], f_send.at[h]))
        for k in range(nz):
            other = lax.rem(z - k + nz, nz) * 2 + 1 - c
            pltpu.make_async_copy(xin.at[h, other], xin.at[h, other], f_recv.at[h, k]).wait()
        for i in range(4):
            x = xin[h, pl.ds(i * pieces, pieces)].astype(F32).reshape(rows, HC).astype(BF16)
            t = tn(x, ein[pl.ds(i * rows, rows), :])
            if i == 0:
                acc[pl.ds(h * HC, HC), :] = t
            elif i < 3:
                acc[pl.ds(h * HC, HC), :] += t
            else:
                t = acc[pl.ds(h * HC, HC), :] + t
                pin_s[h] = t.reshape(pin_s.shape[1:]).astype(BF16)
        scatter(nb, bpeer, bdev, bfar, pin_s.at[h], pin_r.at[h], (2, 1)[h])

    split = len(order) - sum(len(near) + (j in beyond) for j in jumps)
    take_in(0, order[:split])
    out_sum = gather_in(po_z, po_l, po_a, po_r, p_recv, q_send, q_recv)
    take_in(1, order[:split])
    take_in(0, order[split:])
    loads[3].wait()
    input_rows(0)
    take_in(1, order[split:])
    ro[c * nz + z] = roots(out_sum, po_r, q_recv)
    slot_ro = slot_of(ro)
    launch(slot_ro, 3, h_recv)
    input_rows(1)

    for h in range(2):
        arrived(nb, pin_r.at[h], (2, 1)[h])
        rin[h, b] = added(nb, pin_s[h, b], pin_r.at[h]).astype(BF16)
        spread(nb, bdev, bfar, rin.at[h], b, (4, 25)[h])
        if h == 0:
            relay(slot_ro, ro, 3, h_recv)

    landed(ro, 3)
    to_mate(ro.at[pl.ds(c * nz, nz)], ro.at[pl.ds(c * nz, nz)], 5)
    wait_bytes(ro.at[pl.ds(0, nz)], recvs.at[5])

    rows_out = eout.shape[0]
    cols_in = ein.shape[1]
    step = 128
    per = sk_s.shape[1]
    per_block = step // per
    blocks = nz // per_block
    for h in range(2):
        arrived(nb, rin.at[h], (4, 25)[h])
        rotin = rin[h].astype(F32).reshape(HC, cols_in).astype(BF16)
        for g in range(2):
            who = 1 - c if g == 0 else c
            for i in range(blocks):
                slot = who * nz + i * per_block
                at = pl.multiple_of(slot * per, step)
                block = ro[pl.ds(slot, per_block)].reshape(step, QC).astype(F32)
                block = block[:, h * HC : (h + 1) * HC]
                lane = lax.div(iota(block.shape, 1), LQ)
                total = None
                for q in range(QUERIES // 2):
                    only = jnp.where(lane == q, block, 0.0).astype(BF16)
                    m = (nn(only, rotin) * wgt[pl.ds(at, step), :]).astype(BF16)
                    mom[2 * h + q, pl.ds(at, step), :] = m
                    t = nn(m, tsel[2 * h + q])
                    total = t if total is None else total + t
                total = total.reshape(per_block, per, QR)
                if h == 0:
                    sk_s[pl.ds(slot, per_block)] = total
                else:
                    sk_s[pl.ds(slot, per_block)] += total
            if h == 1 and g == 0:
                to_mate(sk_s.at[pl.ds((1 - c) * nz, nz)], sk_p, 6)
    wait_bytes(sk_p, recvs.at[6])
    sk_z[...] = (sk_s[pl.ds(c * nz, nz)] + sk_p[...]).astype(BF16)
    scatter(nz, zpeer, zdev, zfar, sk_z, sk_r, 7)
    arrived(nz, sk_r, 7)
    sk[c * nz + z] = added(nz, sk_z[z], sk_r).astype(BF16)
    spread(nz, zdev, zfar, sk, c * nz + z, 8)
    arrived(nz, sk, 8)
    to_mate(sk.at[pl.ds(c * nz, nz)], sk.at[pl.ds(c * nz, nz)], 9)
    wait_bytes(sk.at[pl.ds(0, nz)], recvs.at[9])

    sketch = sk[...].reshape(rows_out, QR).astype(F32).T.astype(BF16)
    gram = nt(sketch, sketch)
    lane_q = lax.div(iota((RANK, QR), 1), RANK)
    mine = jnp.zeros((RANK, QR), F32)
    for q in range(QUERIES):
        mine = mine + jnp.where(lane_q == q, gram[q * RANK : (q + 1) * RANK, :], 0.0)
    gm_s[...] = mine
    for k in bfar:
        put(gm_s, gm_r.at[k], sends.at[10], recvs.at[10], bdev(k))
    sent.append((gm_r.at[pl.ds(0, nb - 1)], sends.at[10]))

    raw = jnp.concatenate(
        [nn(sketch[q * RANK : (q + 1) * RANK, :], mom[q]) for q in range(QUERIES)], axis=0
    )
    acc[pl.ds(0, QR), :] = raw
    left_raw = nn(sketch, eout[...])

    arrived(nb, gm_r, 10)
    a0 = added(nb, mine, gm_r)
    group = 8
    spot = iota((group, QR), 0)
    lane_t = lax.div(iota((group, QR), 1), RANK)
    in_q = iota((group, QR), 1) - lane_t * RANK

    def over_lanes(x):
        out = None
        for q in range(QUERIES):
            s = jnp.sum(jnp.where(lane_t == q, x, 0.0), axis=1, keepdims=True)
            out = jnp.broadcast_to(s, x.shape) if out is None else jnp.where(lane_t == q, s, out)
        return out

    tiles = RANK // group
    a = [a0[t * group : (t + 1) * group, :] for t in range(tiles)]
    e = [jnp.where(in_q == spot + t * group, 1.0, 0.0).astype(F32) for t in range(tiles)]
    for k in range(RANK):
        first, at = k // group, k % group
        col = [over_lanes(jnp.where(in_q == k, a[t], 0.0)) for t in range(first, tiles)]
        pivot = 1.0 / col[0][at : at + 1, :]
        row_a = a[first][at : at + 1, :] * pivot
        row_e = e[first][at : at + 1, :] * pivot
        for t in range(first, tiles):
            f = col[t - first]
            if t == first:
                f = jnp.where(spot > at, f, 0.0)
            a[t] = a[t] - f * row_a
            e[t] = e[t] - f * row_e
    inv = jnp.concatenate(
        [
            e[t] / jnp.sqrt(over_lanes(jnp.where(in_q == spot + t * group, a[t], 0.0)))
            for t in range(tiles)
        ],
        axis=0,
    )
    tall = jnp.concatenate([inv] * QUERIES, axis=0)
    same = lax.div(iota((QR, QR), 0), RANK) == lax.div(iota((QR, QR), 1), RANK)
    solve = jnp.where(same, tall, 0.0)

    pjs, pjr, pjo = (pj_s0, pj_s1), (pj_r0, pj_r1), (pj0, pj1)
    wide0 = pj_s0.shape[2]
    parts_of = (pl.ds(0, wide0), pl.ds(wide0, cols_in - wide0))
    for h in range(2):
        ortho = nn(solve, acc[pl.ds(0, QR), parts_of[h]], HIGHEST)
        pjs[h][...] = ortho.reshape(pjs[h].shape).astype(BF16)
        scatter(nb, bpeer, bdev, bfar, pjs[h], pjr[h], (11, 26)[h])
    lf_s[...] = nn(solve, left_raw, HIGHEST).T.reshape(lf_s.shape).astype(BF16)
    scatter(nb, bpeer, bdev, bfar, lf_s, lf_r, 12)
    for h in range(2):
        arrived(nb, pjr[h], (11, 26)[h])
        pjo[h][b] = added(nb, pjs[h][b], pjr[h]).astype(BF16)
        spread(nb, bdev, bfar, pjo[h], b, (13, 27)[h])
    arrived(nb, lf_r, 12)
    left_here = added(nb, lf_s[b], lf_r).astype(BF16)
    lf_c[...] = left_here

    @pl.when(b == z)
    def _():
        lf[c * nz + z] = left_here

    @pl.when(b != z)
    def _():
        put(lf_c, lf.at[c * nz + b], sends.at[14], recvs.at[14], twin)

    slots = nz // 2
    tall_rows = slots * rt_s.shape[1]
    for h in range(2):
        arrived(nb, pjo[h], (13, 27)[h])
        proj = pjo[h][...].astype(F32).reshape(QR, -1).astype(BF16)
        for g in range(4):
            slot = (1 - c if g < 2 else c) * nz + (g % 2) * slots
            at = pl.multiple_of(slot * rt_s.shape[1], tall_rows)
            r = nt(ein[pl.ds(at, tall_rows), parts_of[h]], proj).reshape(slots, rt_s.shape[1], QR)
            if h == 0:
                rt_s[pl.ds(slot, slots)] = r
            else:
                rt_s[pl.ds(slot, slots)] += r
            if h == 1 and g == 1:
                to_mate(rt_s.at[pl.ds((1 - c) * nz, nz)], rt_p, 15)
    wait_bytes(rt_p, recvs.at[15])
    rt_z[...] = (rt_s[pl.ds(c * nz, nz)] + rt_p[...]).astype(BF16)
    leaves(rt_z, rt_l, l_send, l_recv)

    @pl.when(b != z)
    def _():
        wait_bytes(lf_c, recvs.at[14])
        wait_bytes(lf_c, sends.at[14])

    slot_lf = slot_of(lf)
    launch(slot_lf, 17, k_recv)
    own = gather_in(rt_z, rt_l, rt_a, rt_r, l_recv, j_send, j_recv)
    relay(slot_lf, lf, 17, k_recv)
    rt[c * nz + z] = roots(own, rt_r, j_recv)
    slot_rt = slot_of(rt)
    launch(slot_rt, 18, g_recv)
    relay(slot_rt, rt, 18, g_recv)
    landed(lf, 17)
    to_mate(lf.at[pl.ds(c * nz, nz)], lf.at[pl.ds(c * nz, nz)], 19)
    landed(rt, 18)
    to_mate(rt.at[pl.ds(c * nz, nz)], rt.at[pl.ds(c * nz, nz)], 20)

    loads[6].wait()
    loads[7].wait()
    loads[8].wait()
    half = act.shape[1] // 2
    tokens = act.shape[0]

    def token_half(who):
        right = rt[pl.ds(who * nz, nz)].astype(F32).reshape(half, QR).astype(BF16)
        return nn(act[:, pl.ds(pl.multiple_of(who * half, half), half)], right)

    tok = token_half(c)
    wait_bytes(lf.at[pl.ds(0, nz)], recvs.at[19])
    left = lf[...].astype(F32).reshape(gr.shape[1], QR).astype(BF16)
    tk_s[:, :, QR:] = nn(gr[...], left).reshape(nb, -1, QR)
    wait_bytes(rt.at[pl.ds(0, nz)], recvs.at[20])
    tok = tok + token_half(1 - c)
    tk_s[:, :, :QR] = tok.reshape(nb, -1, QR)
    scatter(nb, bpeer, bdev, bfar, tk_s, tk_r, 21)

    here = d * tokens + iota((tokens, lens.shape[1]), 0)
    length = lens[...].astype(F32)
    earlier = jnp.where(
        iota((lens.shape[1],) * 2, 0) < iota((lens.shape[1],) * 2, 1), 1.0, 0.0
    ).astype(BF16)
    start = nn(jnp.broadcast_to(length, (8, lens.shape[1])).astype(BF16), earlier)[0:1, :]
    stop = start + length
    place = here.astype(F32)
    member = jnp.where((place >= start) & (place < stop), 1.0, 0.0).astype(F32)
    pick = jnp.where(
        lax.div(iota((QR, 128), 0), RANK) == iota((QR, 128), 1), 1.0, 0.0
    ).astype(F32)

    arrived(nb, tk_r, 21)
    both = added(nb, tk_s[b], tk_r)
    sc[b] = nn(both[:, :QR] * both[:, QR:], pick, HIGHEST)
    spread(nb, bdev, bfar, sc, b, 22)
    arrived(nb, sc, 22)
    every = sc[...].reshape(tokens, 128)
    scores_o[...] = every.T[:QUERIES, :]
    dc_s[...] = tn(every, member, HIGHEST)[0:QUERIES, :]
    to_mate(dc_s, dc_p, 23)
    wait_bytes(dc_p, recvs.at[23])
    dc_z[...] = dc_s[...] + dc_p[...]
    for k in zfar:
        put(dc_z, dc_r.at[k], sends.at[24], recvs.at[24], zdev(k))
    sent.append((dc_r.at[pl.ds(0, nz - 1)], sends.at[24]))
    arrived(nz, dc_r, 24)
    docs = added(nz, dc_z[...], dc_r)
    doc_o[...] = docs
    for ref, sem in sent:
        wait_bytes(ref, sem)


def local(nb, nz, eig_in, eig_out, eigvals, out_factors, in_factors, test_matrix, activations, gradients, doc_lengths):
    ra, cj = eig_in.shape
    ri, ca = eig_out.shape
    tokens = activations.shape[0]
    docs = doc_lengths.shape[0]
    nd = 2 * nz
    vm = pltpu.VMEM
    wide = (cj // 2 + 127) // 128 * 128
    scratch = [
        vm((ra, cj), BF16),
        vm((ri, ca), BF16),
        vm((ri, cj), BF16),
        vm(out_factors.shape, BF16),
        vm((RANK, cj), BF16),
        vm(activations.shape, BF16),
        vm(gradients.shape, BF16),
        vm((1, docs), jnp.int32),
        vm((2, nd, ra // nd, HC), BF16),
        vm((QC, cj), F32),
        vm((ri, cj), F32),
        vm((QUERIES, cj, QR), BF16),
        vm((QUERIES, ri, cj), BF16),
        vm((2, nb, HC // nb, cj), BF16),
        vm((2, nb, HC // nb, cj), BF16),
        vm((2, nb, HC // nb, cj), BF16),
        vm((nd, ri // nd, QC), F32),
        vm((nz, ri // nd, QC), F32),
        vm((nz, ri // nd, QC), BF16),
        vm((15, ri // nd, QC), BF16),
        vm((4, ri // nd, QC), BF16),
        vm((4, ri // nd, QC), BF16),
        vm((nd, ri // nd, QC), BF16),
        vm((nd, ri // nd, QR), F32),
        vm((nz, ri // nd, QR), F32),
        vm((nz, ri // nd, QR), BF16),
        vm((nz, ri // nd, QR), BF16),
        vm((nd, ri // nd, QR), BF16),
        vm((RANK, QR), F32),
        vm((nb, RANK, QR), F32),
        *(vm((nb, QR // nb, w), BF16) for _ in range(3) for w in (wide, cj - wide)),
        vm((nb, ca // nb, QR), BF16),
        vm((nb, ca // nb, QR), BF16),
        vm((ca // nb, QR), BF16),
        vm((nd, ca // nb, QR), BF16),
        vm((nd, ra // nd, QR), F32),
        vm((nz, ra // nd, QR), F32),
        vm((nz, ra // nd, QR), BF16),
        vm((15, ra // nd, QR), BF16),
        vm((4, ra // nd, QR), BF16),
        vm((4, ra // nd, QR), BF16),
        vm((nd, ra // nd, QR), BF16),
        vm((nb, tokens // nb, 2 * QR), F32),
        vm((nb, tokens // nb, 2 * QR), F32),
        vm((nb, tokens // nb, 128), F32),
        vm((QUERIES, docs), F32),
        vm((QUERIES, docs), F32),
        vm((QUERIES, docs), F32),
        vm((nz, QUERIES, docs), F32),
        pltpu.SemaphoreType.DMA((10,)),
        pltpu.SemaphoreType.DMA((2,)),
        pltpu.SemaphoreType.DMA((2, nz)),
        pltpu.SemaphoreType.DMA((2,)),
        pltpu.SemaphoreType.DMA((2, nz)),
        pltpu.SemaphoreType.DMA(()),
        pltpu.SemaphoreType.DMA((5,)),
        pltpu.SemaphoreType.DMA(()),
        pltpu.SemaphoreType.DMA(()),
        pltpu.SemaphoreType.DMA((4,)),
        pltpu.SemaphoreType.DMA(()),
        pltpu.SemaphoreType.DMA((5,)),
        pltpu.SemaphoreType.DMA(()),
        pltpu.SemaphoreType.DMA(()),
        pltpu.SemaphoreType.DMA((4,)),
        pltpu.SemaphoreType.DMA((4,)),
        pltpu.SemaphoreType.DMA((28,)),
        pltpu.SemaphoreType.DMA((28,)),
    ]
    scores, influence = pl.pallas_call(
        functools.partial(body, nb, nz),
        out_shape=(
            jax.ShapeDtypeStruct((QUERIES, tokens), F32),
            jax.ShapeDtypeStruct((QUERIES, docs), F32),
        ),
        in_specs=[pl.BlockSpec(memory_space=pl.ANY)] * 9,
        out_specs=(pl.BlockSpec(memory_space=pltpu.VMEM), pl.BlockSpec(memory_space=pltpu.VMEM)),
        scratch_shapes=scratch,
        compiler_params=pltpu.CompilerParams(
            collective_id=0, has_side_effects=True, vmem_limit_bytes=60 * 1024 * 1024
        ),
        name="influence",
    )(
        eig_in,
        eig_out,
        eigvals,
        out_factors,
        in_factors,
        test_matrix.T,
        activations,
        gradients,
        doc_lengths.reshape(1, docs),
    )
    def leave(a, b, x, y):
        x[...] = a[...]
        y[...] = b[...]

    scores, influence = pl.pallas_call(
        leave,
        out_shape=(
            jax.ShapeDtypeStruct(scores.shape, F32),
            jax.ShapeDtypeStruct(influence.shape, F32),
        ),
        name="leave",
    )(scores, influence)
    return scores.T, influence.T


def solution(mesh):
    nb = mesh.shape["basis"]
    nz = mesh.shape["docs"] // 2
    return jax.shard_map(
        functools.partial(local, nb, nz),
        mesh=mesh,
        in_specs=(
            P("basis", "docs"),
            P("basis", "docs"),
            P("basis", "docs"),
            P("docs", None),
            P(("basis", "docs"), None),
            P("docs", None),
            P("docs", "basis"),
            P("docs", "basis"),
            P(),
        ),
        out_specs=(P("docs", None), P()),
        check_vma=False,
    )
```
